256 devices in a mesh: tm: 32 (over y, x, core), rows: 8 (over z).
Axes of the slice: x: 4, y: 4, z: 8, core: 2. Of those that a mesh axis runs over, the one named last changes fastest.
Arguments:
- frames: bfloat16 [512, 8, 128, 128], P('tm', 'rows'), may hold values from 0.25 to 4
- block_owner: int32 [8, 128, 1], replicated, may hold values from 0 to 31; in each aligned block of 128 rows (0 to 127, 128 to 255, ..., all dimensions but the last counted through in order) at most 12 rows name the same one
- cycle_slot: int32 [8, 128], replicated, may hold values from 0 to 1
- lag_table: int32 [4, 8], replicated, may hold values from 1 to 8
Outputs:
- g2: float32 [8, 32, 128, 128], P('rows', None, 'tm')
- two_time: float32 [512, 64, 512], P('rows', 'tm')
The draws below stay inside these ranges and needn't reach their ends.
Inputs may be any that keep to these rules, and one draw needn't show every extreme that they name: `block_owner`: in each row group no owner gets more than 12 blocks; some owner gets exactly 12 in some groups.
All inputs are finite; a program needn't handle non-finite values.
Results may differ from the reference program's by a relative error of at most 0.0003.
Values may be sent and summed in bfloat16 or wider, within the bound.
A program may use at most 64 MiB of HBM per device.

```python
import math
import jax
import jax.numpy as jnp
import numpy as np
from jax import lax

BLK_DEV = 128
PIX = 128
CYCLES = 64
LEVELS = 4
NLAG = 8
LAGMAX = 8
FRAMES = 512
ROW_GROUPS = 8
CAP = 12
N_TM = 32


def place_ends(result, own_key, least, high):
    place = [jax.random.randint(jax.random.fold_in(own_key, axis), (), 0, length) for axis, length in enumerate(result.shape)]
    widest = result.shape.index(max(result.shape))
    neighbour = place[:widest] + [(place[widest] + 1) % result.shape[widest]] + place[widest + 1:]
    return result.at[tuple(place)].set(least).at[tuple(neighbour)].set(high)


def block_scale(stream_key, dims, shards, least, high):
    loudness, own = 1.0, jax.random.fold_in(stream_key, 6)
    for dim, shards_of in shards:
        heights = jnp.exp(jax.random.uniform(jax.random.fold_in(own, dim), (shards_of,), jnp.float32, least / len(shards), high / len(shards)))
        loudness = loudness * jnp.repeat(heights, dims[dim] // shards_of).reshape([-1 if axis == dim else 1 for axis in range(len(dims))])
    return loudness


def shared_out(key, own, number, rows, count, top, reach, slope):
    order = jax.random.permutation(key, count)
    crowded, common = shares(count, rows * top, reach, slope, True), shares(count, rows * top, reach, slope, False)
    places = jnp.arange(count)

    def named(tallies, rotation):
        used = int((tallies > 0).sum())
        fixed = max(1, used // 4)
        moved = fixed + (places - fixed + rotation * (used - fixed)) % max(1, count - fixed)
        return jnp.zeros((count,), jnp.int32).at[order[jnp.where(places < fixed, places, moved)]].set(jnp.asarray(tallies, jnp.int32))

    tallies = jnp.where(number % 4 == 0, named(crowded, number // 4), named(common, number - number // 4 - 1))
    mixed = jax.random.permutation(jax.random.fold_in(own, 3), count)
    giver, taker = mixed[0:count // 2 * 2:2], mixed[1:count // 2 * 2:2]
    slack = jnp.minimum(tallies[giver] - 1, reach - tallies[taker]) // 2
    slack = jnp.where((giver == order[0]) | (taker == order[0]) | (tallies[taker] == 0), 0, jnp.maximum(slack, 0))
    moved = jax.random.randint(jax.random.fold_in(own, 4), (count // 2,), 0, 1 << 20) % (slack + 1)
    tallies = tallies.at[giver].add(-moved).at[taker].add(moved)
    labels = jnp.searchsorted(jnp.cumsum(tallies), jnp.arange(rows * top), side="right").astype(jnp.int32)
    table = labels.reshape(top, rows).T
    table = table[jax.random.permutation(jax.random.fold_in(own, 1), rows)]
    rotation = jax.random.randint(jax.random.fold_in(own, 2), (rows, 1), 0, top)
    return jnp.take_along_axis(table, (jnp.arange(top)[None, :] + rotation) % top, axis=1)


def shares(count, total, most, skew, full):
    portions = [(1 << 20) // math.isqrt(rank ** skew) + 1 for rank in range(1, count + 1)]
    largest = most if full else min(most, max(-(-total // count), total * portions[0] // sum(portions)))
    least = 1 if total - largest >= count - 1 else 0
    given, rest = [largest] + [least] * (count - 1), total - largest - least * (count - 1)
    while rest > 0:
        movable = [i for i in range(1, count) if given[i] < largest] or [i for i in range(1, count) if given[i] < most]
        whole, remaining = sum([portions[i] for i in movable]), rest
        for i in movable:
            more = min(most - given[i], max(1, remaining * portions[i] // whole), rest)
            given[i] = given[i] + more
            rest = rest - more
    return np.array(given)


def setup_inputs(seed: int = 0) -> dict:
    key_of = jax.random.split(jax.random.key(seed), 5)
    frames = jnp.clip(jnp.exp(math.log(4.0) - 2.7725887 * jax.random.uniform(key_of[0], (FRAMES, ROW_GROUPS, BLK_DEV, PIX), jnp.float32) ** block_scale(key_of[0], (FRAMES, ROW_GROUPS, BLK_DEV, PIX), ((0, 32), (1, 8)), -0.2, 0.2)), 0.25, 4.0).astype(jnp.bfloat16)
    block_owner_keys = jax.random.split(jax.random.fold_in(key_of[1], 1), ROW_GROUPS * BLK_DEV // BLK_DEV)
    block_owner_turns = jax.random.permutation(jax.random.fold_in(key_of[1], 3), ROW_GROUPS * BLK_DEV // BLK_DEV)
    block_owner = jax.vmap(lambda own, number: shared_out(jax.random.fold_in(key_of[1], 2), own, number, BLK_DEV, N_TM, 1, CAP, 2))(block_owner_keys, block_owner_turns).reshape((ROW_GROUPS, BLK_DEV, 1))
    cycle_slot = place_ends(jax.random.randint(key_of[2], (ROW_GROUPS, BLK_DEV), 0, CYCLES // N_TM), jax.random.fold_in(key_of[2], 1), 0, (CYCLES // N_TM) - 1).astype(jnp.int32)
    lag_table = place_ends(jax.random.randint(key_of[3], (LEVELS, NLAG), 1, LAGMAX + 1), jax.random.fold_in(key_of[3], 1), 1, LAGMAX).astype(jnp.int32)
    return dict(frames=frames, block_owner=block_owner, cycle_slot=cycle_slot, lag_table=lag_table)


def multitau(series, lag_table):
    results = []
    current = series
    for level in range(LEVELS):
        length = current.shape[0]
        padded = jnp.concatenate([current, jnp.zeros((LAGMAX,) + current.shape[1:], current.dtype)], 0)
        positions = jnp.arange(length, dtype=jnp.int32)

        def single_lag(lag, current=current, padded=padded, length=length, positions=positions):
            shifted = lax.dynamic_slice_in_dim(padded, lag, length, 0).astype(jnp.float32)
            base = current.astype(jnp.float32)
            valid = (positions < length - lag)[:, None, None]
            count = (length - lag).astype(jnp.float32)
            first = jnp.sum(jnp.where(valid, base, jnp.float32(0.0)), 0)
            second = jnp.sum(shifted, 0)
            product = jnp.sum(jnp.where(valid, base * shifted, jnp.float32(0.0)), 0)
            denom = first * second
            safe = jnp.where(denom > 0, denom, jnp.float32(1.0))
            return jnp.where(denom > 0, product * count / safe, jnp.float32(0.0))

        results.append(lax.map(single_lag, lag_table[level]))
        if level + 1 < LEVELS:
            base = current.astype(jnp.float32)
            current = (base[0::2] + base[1::2]) * 0.5
    return jnp.concatenate(results, 0)


def reference(frames, block_owner, cycle_slot, lag_table):
    nframes, groups, blocks = frames.shape[0], frames.shape[1], frames.shape[2]
    cycle_dev = CYCLES // N_TM
    cycles = (block_owner[:, :, 0] * cycle_dev + cycle_slot).astype(jnp.int32)

    def group_corr(group):
        return multitau(lax.dynamic_index_in_dim(frames, group, 1, False), lag_table)

    g2 = lax.map(group_corr, jnp.arange(groups, dtype=jnp.int32))

    def group_gram(total, group):
        xgroup = lax.dynamic_index_in_dim(frames, group, 1, False)
        row_group = lax.dynamic_index_in_dim(cycles, group, 0, False)

        def add_block(part, block):
            xblock = lax.dynamic_index_in_dim(xgroup, block, 1, False)
            term = jnp.dot(xblock, xblock.T, preferred_element_type=jnp.float32)
            target = row_group[block].astype(jnp.int32)
            current = lax.dynamic_index_in_dim(part, target, 0, False)
            return lax.dynamic_update_index_in_dim(part, current + term, target, 0), None

        part, _ = lax.scan(add_block, jnp.zeros((CYCLES, nframes, nframes), jnp.float32), jnp.arange(blocks, dtype=jnp.int32))
        return total + part, None

    gram, _ = lax.scan(group_gram, jnp.zeros((CYCLES, nframes, nframes), jnp.float32), jnp.arange(groups, dtype=jnp.int32))
    onehot = (cycles[:, :, None] == jnp.arange(CYCLES, dtype=jnp.int32)[None, None, :]).astype(jnp.float32)
    block_totals = jnp.sum(frames.astype(jnp.float32), 3)
    sums = jnp.einsum('fgb,gbr->rf', block_totals, onehot, precision=lax.Precision.HIGHEST)
    counts = PIX * jnp.sum(onehot, (0, 1))
    denom = jnp.maximum(sums.T[:, :, None] * sums[None, :, :], jnp.float32(1.0))
    two_time = counts[None, :, None] * jnp.transpose(gram, (1, 0, 2)) / denom
    return g2, two_time
```

```python
import functools

import jax
import jax.numpy as jnp
from jax import lax
from jax.experimental import pallas as pl
from jax.experimental.pallas import tpu as pltpu
from jax.sharding import PartitionSpec as P

CYCLES = 64
LEVELS = 4
LAGMAX = 8
MESH = pl.DeviceIdType.MESH
FLOWS = ((0, 1, 4), (1, -1, 4), (0, -1, 3), (1, 1, 3))
STEPS = 4
CODE = 14500.0
BIAS = 32767


def pack(slot_ref, x_ref, out_ref):
    out_ref[...] = jnp.zeros_like(out_ref)

    def place(b, carry):
        out_ref[slot_ref[b]] = x_ref[b]
        return carry

    lax.fori_loop(0, x_ref.shape[0], place, 0, unroll=8)


def multitau_block(b, recv_ref, pad_ref, level_ref, table_ref):
    nf = recv_ref.shape[0] * recv_ref.shape[2]
    width = recv_ref.shape[3]
    pad_ref[pl.ds(0, nf), :] = recv_ref[:, b].astype(jnp.float32).reshape(nf, width)
    sub = lax.broadcasted_iota(jnp.int32, (8, width), 0)
    for level in range(LEVELS):
        length = nf >> level
        cols = length // 8

        def get(q, level=level, cols=cols):
            if level == 0:
                return pad_ref[pl.ds(q, 8, stride=cols), :]
            return level_ref[level - 1, q]

        window = [get(q) for q in range(LAGMAX)]
        products = [None] * LAGMAX
        total = None
        heads = []
        tails = [None] * LAGMAX
        previous = None
        for q in range(cols):
            window.append(get(q + LAGMAX))
            base = window[q]
            total = base if total is None else total + base
            if q < LAGMAX:
                heads.append(base[0:1])
            if q >= cols - LAGMAX:
                tails[cols - 1 - q] = base[7:8]
            for d in range(1, LAGMAX + 1):
                term = base * window[q + d]
                products[d - 1] = term if products[d - 1] is None else products[d - 1] + term
            if level + 1 < LEVELS:
                if q % 2 == 0:
                    previous = base
                else:
                    mean = (previous + base) * 0.5
                    level_ref[level, q // 2] = mean
                    if q // 2 < LAGMAX:
                        halo = jnp.where(sub < 7, pltpu.roll(mean, 7, 0), 0.0)
                        level_ref[level, cols // 2 + q // 2] = halo
        whole = jnp.sum(total, 0, keepdims=True)
        first, second = whole, whole
        for d in range(1, LAGMAX + 1):
            first = first - tails[d - 1]
            second = second - heads[d - 1]
            product = jnp.sum(products[d - 1], 0, keepdims=True)
            denom = first * second
            safe = jnp.where(denom > 0, denom, 1.0)
            value = jnp.where(denom > 0, product * float(length - d) / safe, 0.0)
            table_ref[level * LAGMAX + d - 1, pl.ds(b, 1), :] = value


def core(
    ntm,
    nrows,
    lag_ref,
    count_ref,
    mask_ref,
    wide_ref,
    near_ref,
    g2_ref,
    two_ref,
    wide_in,
    near_in,
    pad_ref,
    level_ref,
    table_ref,
    gram_ref,
    sums_ref,
    tall_ref,
    out_buf,
    in_buf,
    local_sem,
    wide_send,
    wide_recv,
    near_send,
    near_recv,
    sum_send,
    sum_recv,
    ring_send,
    ring_recv,
):
    me = lax.axis_index("tm")
    row = lax.axis_index("rows")
    barrier = pltpu.get_barrier_semaphore()

    def hello_tm(i, carry):
        peer = lax.rem(me + i, ntm)
        pl.semaphore_signal(barrier, inc=1, device_id=(peer, row), device_id_type=MESH)
        return carry

    def hello_rows(i, carry):
        peer = lax.rem(row + i, nrows)
        pl.semaphore_signal(barrier, inc=1, device_id=(me, peer), device_id_type=MESH)
        return carry

    lax.fori_loop(1, ntm, hello_tm, 0)
    lax.fori_loop(1, nrows, hello_rows, 0)
    own_wide = pltpu.make_async_copy(wide_ref.at[me], wide_in.at[me], local_sem.at[0])
    own_near = pltpu.make_async_copy(near_ref.at[me], near_in.at[me], local_sem.at[1])
    own_wide.start()
    own_near.start()
    pad_ref[...] = jnp.zeros_like(pad_ref)
    pl.semaphore_wait(barrier, ntm + nrows - 2)

    def wide_copy(i):
        peer = lax.rem(me + i, ntm)
        return pltpu.make_async_remote_copy(
            src_ref=wide_ref.at[peer],
            dst_ref=wide_in.at[me],
            send_sem=wide_send.at[i],
            recv_sem=wide_recv.at[me],
            device_id=(peer, row),
            device_id_type=MESH,
        )

    def near_copy(i):
        peer = lax.rem(me + i, ntm)
        return pltpu.make_async_remote_copy(
            src_ref=near_ref.at[peer],
            dst_ref=near_in.at[me],
            send_sem=near_send.at[i],
            recv_sem=near_recv.at[me],
            device_id=(peer, row),
            device_id_type=MESH,
        )

    def arrival(buf, sem, i):
        peer = lax.rem(me + ntm - i, ntm)
        return pltpu.make_async_remote_copy(
            src_ref=buf.at[peer],
            dst_ref=buf.at[peer],
            send_sem=sem.at[peer],
            recv_sem=sem.at[peer],
            device_id=(peer, row),
            device_id_type=MESH,
        )

    def each(body):
        def step(i, carry):
            body(i)
            return carry

        lax.fori_loop(1, ntm, step, 0)

    each(lambda i: wide_copy(i).start())
    each(lambda i: near_copy(i).start())
    own_wide.wait()
    each(lambda i: arrival(wide_in, wide_recv, i).wait_recv())

    slots = wide_in.shape[1]
    nf = ntm * wide_in.shape[2]
    width = wide_in.shape[3]
    span = nf // nrows
    pixels = jnp.concatenate([wide_in[:, k].reshape(nf, width) for k in range(slots)], 1)
    contract = (((1,), (1,)), ((), ()))
    sums_ref[row] = lax.dot_general(
        mask_ref[...], pixels, contract, preferred_element_type=jnp.float32
    )

    def sum_copy(i):
        peer = lax.rem(row + i, nrows)
        return pltpu.make_async_remote_copy(
            src_ref=sums_ref.at[row],
            dst_ref=sums_ref.at[row],
            send_sem=sum_send.at[i],
            recv_sem=sum_recv.at[row],
            device_id=(me, peer),
            device_id_type=MESH,
        )

    def sum_arrival(i):
        peer = lax.rem(row + nrows - i, nrows)
        return pltpu.make_async_remote_copy(
            src_ref=sums_ref.at[peer],
            dst_ref=sums_ref.at[peer],
            send_sem=sum_recv.at[peer],
            recv_sem=sum_recv.at[peer],
            device_id=(me, peer),
            device_id_type=MESH,
        )

    for i in range(1, nrows):
        sum_copy(i).start()
    for a in range(2):
        gram_ref[a] = lax.dot_general(
            pixels * mask_ref[a : a + 1, :], pixels, contract, preferred_element_type=jnp.float32
        )
    for i in range(1, nrows):
        sum_arrival(i).wait_recv()
    sums = sums_ref[0]
    for i in range(1, nrows):
        sums = sums + sums_ref[i]
    tall_ref[...] = sums.T

    def own_part(a, slab):
        start = pl.multiple_of(slab * span, span)
        first = tall_ref[pl.ds(start, span), a : a + 1]
        denom = jnp.maximum(first * sums[a : a + 1, :], 1.0)
        return gram_ref[a, pl.ds(start, span), :] * (count_ref[a] / denom)

    def ring_copy(flow, step):
        _, way, hops = FLOWS[flow]
        return pltpu.make_async_remote_copy(
            src_ref=out_buf.at[flow, step],
            dst_ref=in_buf.at[flow, step],
            send_sem=ring_send.at[flow, step],
            recv_sem=ring_recv.at[flow, step],
            device_id=(me, lax.rem(row + way + nrows, nrows)),
            device_id_type=MESH,
        )

    def tau(b, carry):
        multitau_block(b, near_in, pad_ref, level_ref, table_ref)
        return carry

    for step in range(STEPS):
        for flow, (a, way, hops) in enumerate(FLOWS):
            if step >= hops:
                continue
            slab = lax.rem(row + way * (hops - step) + nrows, nrows)
            code = (own_part(a, slab) * CODE + 0.5).astype(jnp.int32)
            if step:
                ring_copy(flow, step - 1).wait_recv()
                code = code + in_buf[flow, step - 1].astype(jnp.int32)
            else:
                code = code - BIAS
            out_buf[flow, step] = code.astype(jnp.int16)
            ring_copy(flow, step).start()
        if step == 0:
            own_near.wait()
            each(lambda i: arrival(near_in, near_recv, i).wait_recv())
        lax.fori_loop(step, step + 1, tau, 0)

    for l in range(lag_ref.shape[0]):
        g2_ref[l] = table_ref[(l // LAGMAX) * LAGMAX + lag_ref[l]]
    total = [own_part(a, row) for a in range(2)]
    for flow, (a, way, hops) in enumerate(FLOWS):
        ring_copy(flow, hops - 1).wait_recv()
        code = in_buf[flow, hops - 1].astype(jnp.int32) + BIAS
        total[a] = total[a] + code.astype(jnp.float32) * (1.0 / CODE)
    for a in range(2):
        two_ref[a] = total[a]

    each(lambda i: wide_copy(i).wait_send())
    each(lambda i: near_copy(i).wait_send())
    for i in range(1, nrows):
        sum_copy(i).wait_send()
    for flow, (a, way, hops) in enumerate(FLOWS):
        for step in range(hops):
            ring_copy(flow, step).wait_send()


def shards(frames, block_owner, cycle_slot, lag_table):
    local = frames[:, 0]
    span, nblocks, width = local.shape
    ntm = lax.axis_size("tm")
    nrows = lax.axis_size("rows")
    me_tm = lax.axis_index("tm")
    me_row = lax.axis_index("rows")
    cap = 3 * nblocks // ntm
    near = nblocks // ntm
    nf = span * ntm
    owners_all = block_owner[:, :, 0]
    owners = lax.dynamic_index_in_dim(owners_all, me_row, 0, False)
    slots = lax.dynamic_index_in_dim(cycle_slot, me_row, 0, False)
    order = jnp.arange(nblocks, dtype=jnp.int32)
    rank = jnp.sum(
        ((owners[:, None] == owners[None, :]) & (order[None, :] < order[:, None])).astype(jnp.int32), 1
    )
    place = owners * cap + rank
    tall = jnp.swapaxes(local, 0, 1)
    vmem = pl.BlockSpec(memory_space=pltpu.VMEM)
    smem = pl.BlockSpec(memory_space=pltpu.SMEM)
    wide = pl.pallas_call(
        pack,
        out_shape=jax.ShapeDtypeStruct((ntm * cap, span, width), local.dtype),
        in_specs=[smem, vmem],
        out_specs=vmem,
    )(place, tall)
    lane_slot = jnp.arange(cap * width, dtype=jnp.int32) // width
    hit = (place[:, None] == me_tm * cap + lane_slot[None, :])[None] & (
        slots[None, :] == jnp.arange(8, dtype=jnp.int32)[:, None]
    )[:, :, None]
    masks = jnp.any(hit, 1).astype(jnp.bfloat16)
    cycles_all = owners_all * 2 + cycle_slot
    mine = me_tm * 2 + jnp.arange(2, dtype=jnp.int32)
    counts = width * jnp.sum((cycles_all[:, :, None] == mine).astype(jnp.float32), (0, 1))
    nflow = len(FLOWS)
    out_span = nf // nrows
    dma = pltpu.SemaphoreType.DMA
    g2, two = pl.pallas_call(
        functools.partial(core, ntm, nrows),
        out_shape=(
            jax.ShapeDtypeStruct((LEVELS * 8, near, width), jnp.float32),
            jax.ShapeDtypeStruct((2, out_span, nf), jnp.float32),
        ),
        in_specs=[smem, smem, vmem, vmem, vmem],
        out_specs=(vmem, vmem),
        scratch_shapes=[
            pltpu.VMEM((ntm, cap, span, width), jnp.bfloat16),
            pltpu.VMEM((ntm, near, span, width), jnp.bfloat16),
            pltpu.VMEM((nf + 64, width), jnp.float32),
            pltpu.VMEM((LEVELS - 1, nf // 16 + LAGMAX, 8, width), jnp.float32),
            pltpu.VMEM((LEVELS * LAGMAX, near, width), jnp.float32),
            pltpu.VMEM((2, nf, nf), jnp.float32),
            pltpu.VMEM((nrows, 8, nf), jnp.float32),
            pltpu.VMEM((nf, 8), jnp.float32),
            pltpu.VMEM((nflow, STEPS, out_span, nf), jnp.int16),
            pltpu.VMEM((nflow, STEPS, out_span, nf), jnp.int16),
            dma((2,)),
            dma((ntm,)),
            dma((ntm,)),
            dma((ntm,)),
            dma((ntm,)),
            dma((nrows,)),
            dma((nrows,)),
            dma((nflow, STEPS)),
            dma((nflow, STEPS)),
        ],
        compiler_params=pltpu.CompilerParams(collective_id=0, has_side_effects=True),
    )(
        jnp.clip(lag_table.reshape(-1) - 1, 0, LAGMAX - 1),
        counts,
        masks,
        wide.reshape(ntm, cap, span, width),
        tall.reshape(ntm, near, span, width),
    )
    return g2[None], jnp.swapaxes(two, 0, 1)


def solution(mesh):
    in_specs = (P("tm", "rows", None, None), P(), P(), P())
    out_specs = (P("rows", None, "tm", None), P("rows", "tm", None))
    return jax.shard_map(shards, mesh=mesh, in_specs=in_specs, out_specs=out_specs, check_vma=False)
```

```python
import functools

import jax
import jax.numpy as jnp
from jax import lax
from jax.experimental import pallas as pl
from jax.experimental.pallas import tpu as pltpu
from jax.sharding import PartitionSpec as P

CYCLES = 64
LEVELS = 4
LAGMAX = 8
MESH = pl.DeviceIdType.MESH
FLOWS = ((0, 1, 4), (1, -1, 4), (0, -1, 3), (1, 1, 3))
STEPS = 4
CODE = 14500.0
BIAS = 32767


def multitau_block(b, recv_ref, pad_ref, level_ref, table_ref):
    nf = recv_ref.shape[0] * recv_ref.shape[2]
    width = recv_ref.shape[3]
    pad_ref[pl.ds(0, nf), :] = recv_ref[:, b].astype(jnp.float32).reshape(nf, width)
    sub = lax.broadcasted_iota(jnp.int32, (8, width), 0)
    for level in range(LEVELS):
        length = nf >> level
        cols = length // 8

        def get(q, level=level, cols=cols):
            if level == 0:
                return pad_ref[pl.ds(q, 8, stride=cols), :]
            return level_ref[level - 1, q]

        window = [get(q) for q in range(LAGMAX)]
        products = [None] * LAGMAX
        total = None
        heads = []
        tails = [None] * LAGMAX
        previous = None
        for q in range(cols):
            window.append(get(q + LAGMAX))
            base = window[q]
            total = base if total is None else total + base
            if q < LAGMAX:
                heads.append(base[0:1])
            if q >= cols - LAGMAX:
                tails[cols - 1 - q] = base[7:8]
            for d in range(1, LAGMAX + 1):
                term = base * window[q + d]
                products[d - 1] = term if products[d - 1] is None else products[d - 1] + term
            if level + 1 < LEVELS:
                if q % 2 == 0:
                    previous = base
                else:
                    mean = (previous + base) * 0.5
                    level_ref[level, q // 2] = mean
                    if q // 2 < LAGMAX:
                        halo = jnp.where(sub < 7, pltpu.roll(mean, 7, 0), 0.0)
                        level_ref[level, cols // 2 + q // 2] = halo
        whole = jnp.sum(total, 0, keepdims=True)
        first, second = whole, whole
        for d in range(1, LAGMAX + 1):
            first = first - tails[d - 1]
            second = second - heads[d - 1]
            product = jnp.sum(products[d - 1], 0, keepdims=True)
            denom = first * second
            safe = jnp.where(denom > 0, denom, 1.0)
            value = jnp.where(denom > 0, product * float(length - d) / safe, 0.0)
            table_ref[level * LAGMAX + d - 1, pl.ds(b, 1), :] = value


def far_first(ny, nx):
    offsets = [(dy, dx, dc) for dy in range(ny) for dx in range(nx) for dc in range(2)][1:]
    return sorted(offsets, key=lambda o: -(min(o[0], ny - o[0]) + min(o[1], nx - o[1])))


def core(
    ntm,
    nrows,
    lag_ref,
    owner_ref,
    slot_ref,
    frames_ref,
    g2_ref,
    two_ref,
    raw,
    flat,
    near_out,
    wide_out,
    wide_in,
    near_in,
    table_vec,
    table,
    pad_ref,
    level_ref,
    corr_ref,
    gram_ref,
    sums_ref,
    tall_ref,
    out_buf,
    in_buf,
    local_sem,
    wide_send,
    wide_recv,
    near_send,
    near_recv,
    sum_send,
    sum_recv,
    ring_send,
    ring_recv,
):
    me = lax.axis_index("tm")
    row = lax.axis_index("rows")
    nx = 4
    ny = ntm // (2 * nx)
    barrier = pltpu.get_barrier_semaphore()
    load = pltpu.make_async_copy(frames_ref.at[:, 0], raw, local_sem.at[0])
    load.start()

    def hello_tm(i, carry):
        peer = lax.rem(me + i, ntm)
        pl.semaphore_signal(barrier, inc=1, device_id=(peer, row), device_id_type=MESH)
        return carry

    def hello_rows(i, carry):
        peer = lax.rem(row + i, nrows)
        pl.semaphore_signal(barrier, inc=1, device_id=(me, peer), device_id_type=MESH)
        return carry

    lax.fori_loop(1, ntm, hello_tm, 0)
    lax.fori_loop(1, nrows, hello_rows, 0)

    span, nblocks, width = raw.shape
    slots = wide_in.shape[1]
    near = near_in.shape[1]
    square = (nblocks, nblocks)
    owners = owner_ref[pl.ds(row, 1), :].astype(jnp.float32)
    cycles = slot_ref[pl.ds(row, 1), :].astype(jnp.float32)
    down = lax.broadcasted_iota(jnp.int32, square, 0)
    along = lax.broadcasted_iota(jnp.int32, square, 1)
    alongf = along.astype(jnp.float32)
    across = jnp.broadcast_to(owners, square)
    same = (across == across.T) & (down < along)
    rank = jnp.sum(jnp.where(same, 1.0, 0.0), 0, keepdims=True)
    place = jnp.broadcast_to(owners * float(slots) + rank, square).T
    entry = jnp.broadcast_to(alongf[0:1] + float(nblocks) * (1.0 + cycles), square).T
    parts = ntm * slots // nblocks
    rows_of = [
        jnp.sum(jnp.where(place == alongf + float(j * nblocks), entry, 0.0), 0, keepdims=True)
        for j in range(parts)
    ]
    table_vec[...] = jnp.concatenate(
        rows_of + [jnp.zeros((8 - parts, nblocks), jnp.float32)], 0
    ).astype(jnp.int32)
    fetch = pltpu.make_async_copy(table_vec, table, local_sem.at[1])
    fetch.start()
    pad_ref[...] = jnp.zeros_like(pad_ref)
    load.wait()
    flat[...] = raw[...].astype(jnp.float32).reshape(span * nblocks, width)

    def turn(b, carry):
        near_out[b // near, b % near] = flat[pl.ds(b, span, stride=nblocks), :].astype(jnp.bfloat16)
        return carry

    lax.fori_loop(0, nblocks, turn, 0, unroll=8)
    fetch.wait()

    def entry_at(i):
        return table[i // nblocks, i % nblocks]

    def fill(o, carry):
        for k in range(slots):
            b = entry_at(o * slots + k) % nblocks
            wide_out[o, k] = near_out[b // near, b % near]
        return carry

    lax.fori_loop(0, ntm, fill, 0)
    wide_in[me] = wide_out[me]
    near_in[me] = near_out[me]
    pl.semaphore_wait(barrier, ntm + nrows - 2)

    order = far_first(ny, nx)
    y, x, c = me // (2 * nx), (me // 2) % nx, me % 2

    def peer_at(offset):
        dy, dx, dc = offset
        return (lax.rem(y + dy, ny) * nx + lax.rem(x + dx, nx)) * 2 + lax.rem(c + dc, 2)

    def plane_copy(out, into, send, recv, peer):
        return pltpu.make_async_remote_copy(
            src_ref=out.at[peer],
            dst_ref=into.at[me],
            send_sem=send.at[peer],
            recv_sem=recv.at[me],
            device_id=(peer, row),
            device_id_type=MESH,
        )

    def wide_copy(peer):
        return plane_copy(wide_out, wide_in, wide_send, wide_recv, peer)

    def near_copy(peer):
        return plane_copy(near_out, near_in, near_send, near_recv, peer)

    def arrival(buf, sem, peer):
        return pltpu.make_async_remote_copy(
            src_ref=buf.at[peer],
            dst_ref=buf.at[peer],
            send_sem=sem.at[peer],
            recv_sem=sem.at[peer],
            device_id=(peer, row),
            device_id_type=MESH,
        )

    def each(body):
        def step(i, carry):
            body(lax.rem(me + i, ntm))
            return carry

        lax.fori_loop(1, ntm, step, 0)

    for offset in order:
        wide_copy(peer_at(offset)).start()
    for offset in order:
        near_copy(peer_at(offset)).start()
    each(lambda peer: arrival(wide_in, wide_recv, peer).wait_recv())

    nf = ntm * span
    slab_len = nf // nrows
    pixels = [wide_in[:, k].reshape(nf, width) for k in range(slots)]
    whole = jnp.concatenate(pixels, 1)
    own_entries = [entry_at(me * slots + k) // nblocks for k in range(slots)]
    flags = [
        [jnp.where(e == a + 1, 1.0, 0.0) for e in own_entries] for a in range(2)
    ]
    contract = (((1,), (1,)), ((), ()))
    lines = [
        jnp.concatenate([jnp.full((1, width), f, jnp.float32) for f in flags[a]], 1) for a in range(2)
    ]
    masks = jnp.concatenate(lines + [jnp.zeros((6, slots * width), jnp.float32)], 0)
    masks = masks.astype(jnp.bfloat16)
    sums_ref[row] = lax.dot_general(masks, whole, contract, preferred_element_type=jnp.float32)

    def sum_copy(i):
        peer = lax.rem(row + i, nrows)
        return pltpu.make_async_remote_copy(
            src_ref=sums_ref.at[row],
            dst_ref=sums_ref.at[row],
            send_sem=sum_send.at[i],
            recv_sem=sum_recv.at[row],
            device_id=(me, peer),
            device_id_type=MESH,
        )

    def sum_arrival(i):
        peer = lax.rem(row + nrows - i, nrows)
        return pltpu.make_async_remote_copy(
            src_ref=sums_ref.at[peer],
            dst_ref=sums_ref.at[peer],
            send_sem=sum_recv.at[peer],
            recv_sem=sum_recv.at[peer],
            device_id=(me, peer),
            device_id_type=MESH,
        )

    for i in range(1, nrows):
        sum_copy(i).start()
    for a in range(2):
        gram_ref[a] = lax.dot_general(
            whole * masks[a : a + 1, :], whole, contract, preferred_element_type=jnp.float32
        )
    cycle_all = owner_ref[...] * 2 + slot_ref[...]
    counts = []
    for a in range(2):
        hits = jnp.where(cycle_all == me * 2 + a, float(width), 0.0)
        counts.append(jnp.sum(jnp.sum(hits, 1, keepdims=True), 0, keepdims=True))
    for i in range(1, nrows):
        sum_arrival(i).wait_recv()
    sums = sums_ref[0]
    for i in range(1, nrows):
        sums = sums + sums_ref[i]
    tall_ref[...] = sums.T

    def own_part(a, slab):
        start = pl.multiple_of(slab * slab_len, slab_len)
        first = tall_ref[pl.ds(start, slab_len), a : a + 1]
        denom = jnp.maximum(first * sums[a : a + 1, :], 1.0)
        return gram_ref[a, pl.ds(start, slab_len), :] * (counts[a] / denom)

    def ring_copy(flow, step):
        _, way, hops = FLOWS[flow]
        return pltpu.make_async_remote_copy(
            src_ref=out_buf.at[flow, step],
            dst_ref=in_buf.at[flow, step],
            send_sem=ring_send.at[flow, step],
            recv_sem=ring_recv.at[flow, step],
            device_id=(me, lax.rem(row + way + nrows, nrows)),
            device_id_type=MESH,
        )

    def tau(b, carry):
        multitau_block(b, near_in, pad_ref, level_ref, corr_ref)
        return carry

    for step in range(STEPS):
        for flow, (a, way, hops) in enumerate(FLOWS):
            if step >= hops:
                continue
            slab = lax.rem(row + way * (hops - step) + nrows, nrows)
            code = (own_part(a, slab) * CODE + 0.5).astype(jnp.int32)
            if step:
                ring_copy(flow, step - 1).wait_recv()
                code = code + in_buf[flow, step - 1].astype(jnp.int32)
            else:
                code = code - BIAS
            out_buf[flow, step] = code.astype(jnp.int16)
            ring_copy(flow, step).start()
        if step == 1:
            each(lambda peer: arrival(near_in, near_recv, peer).wait_recv())
        if step >= 1:
            lax.fori_loop((0, 0, 1, 2)[step], (0, 1, 2, 4)[step], tau, 0)

    for l in range(LEVELS):
        for j in range(lag_ref.shape[1]):
            g2_ref[l * lag_ref.shape[1] + j] = corr_ref[
                l * LAGMAX + jnp.maximum(lag_ref[l, j] - 1, 0)
            ]
    total = [own_part(a, row) for a in range(2)]
    for flow, (a, way, hops) in enumerate(FLOWS):
        ring_copy(flow, hops - 1).wait_recv()
        code = in_buf[flow, hops - 1].astype(jnp.int32) + BIAS
        total[a] = total[a] + code.astype(jnp.float32) * (1.0 / CODE)
    for a in range(2):
        two_ref[a] = total[a]

    each(lambda peer: wide_copy(peer).wait_send())
    each(lambda peer: near_copy(peer).wait_send())
    for i in range(1, nrows):
        sum_copy(i).wait_send()
    for flow, (a, way, hops) in enumerate(FLOWS):
        for step in range(hops):
            ring_copy(flow, step).wait_send()


def shards(frames, block_owner, cycle_slot, lag_table):
    span, _, nblocks, width = frames.shape
    ntm = lax.axis_size("tm")
    nrows = lax.axis_size("rows")
    cap = 3 * nblocks // ntm
    near = nblocks // ntm
    nf = span * ntm
    slab = nf // nrows
    nflow = len(FLOWS)
    vmem = pl.BlockSpec(memory_space=pltpu.VMEM)
    smem = pl.BlockSpec(memory_space=pltpu.SMEM)
    dma = pltpu.SemaphoreType.DMA
    bf16, f32, i32, i16 = jnp.bfloat16, jnp.float32, jnp.int32, jnp.int16
    g2, two = pl.pallas_call(
        functools.partial(core, ntm, nrows),
        out_shape=(
            jax.ShapeDtypeStruct((LEVELS * lag_table.shape[1], near, width), f32),
            jax.ShapeDtypeStruct((2, slab, nf), f32),
        ),
        in_specs=[smem, vmem, vmem, pl.BlockSpec(memory_space=pl.ANY)],
        out_specs=(vmem, vmem),
        scratch_shapes=[
            pltpu.VMEM((span, nblocks, width), bf16),
            pltpu.VMEM((span * nblocks, width), f32),
            pltpu.VMEM((ntm, near, span, width), bf16),
            pltpu.VMEM((ntm, cap, span, width), bf16),
            pltpu.VMEM((ntm, cap, span, width), bf16),
            pltpu.VMEM((ntm, near, span, width), bf16),
            pltpu.VMEM((8, nblocks), i32),
            pltpu.SMEM((8, nblocks), i32),
            pltpu.VMEM((nf + 64, width), f32),
            pltpu.VMEM((LEVELS - 1, nf // 16 + LAGMAX, 8, width), f32),
            pltpu.VMEM((LEVELS * LAGMAX, near, width), f32),
            pltpu.VMEM((2, nf, nf), f32),
            pltpu.VMEM((nrows, 8, nf), f32),
            pltpu.VMEM((nf, 8), f32),
            pltpu.VMEM((nflow, STEPS, slab, nf), i16),
            pltpu.VMEM((nflow, STEPS, slab, nf), i16),
            dma((2,)),
            dma((ntm,)),
            dma((ntm,)),
            dma((ntm,)),
            dma((ntm,)),
            dma((nrows,)),
            dma((nrows,)),
            dma((nflow, STEPS)),
            dma((nflow, STEPS)),
        ],
        compiler_params=pltpu.CompilerParams(collective_id=0, has_side_effects=True),
    )(lag_table, block_owner[:, :, 0], cycle_slot, frames)
    return g2[None], jnp.swapaxes(two, 0, 1)


def solution(mesh):
    in_specs = (P("tm", "rows", None, None), P(), P(), P())
    out_specs = (P("rows", None, "tm", None), P("rows", "tm", None))
    return jax.shard_map(shards, mesh=mesh, in_specs=in_specs, out_specs=out_specs, check_vma=False)
```

```python
import functools

import jax
import jax.numpy as jnp
from jax import lax
from jax.experimental import pallas as pl
from jax.experimental.pallas import tpu as pltpu
from jax.sharding import PartitionSpec as P

CYCLES = 64
LEVELS = 4
LAGMAX = 8
MESH = pl.DeviceIdType.MESH
FLOWS = ((0, 1, 4), (1, -1, 4), (0, -1, 3), (1, 1, 3))
STEPS = 4
CODE = 14500.0
BIAS = 32767


def multitau_block(b, recv_ref, pad_ref, level_ref, table_ref):
    nf = recv_ref.shape[0] * recv_ref.shape[2]
    width = recv_ref.shape[3]
    pad_ref[pl.ds(0, nf), :] = recv_ref[:, b].astype(jnp.float32).reshape(nf, width)
    sub = lax.broadcasted_iota(jnp.int32, (8, width), 0)
    for level in range(LEVELS):
        length = nf >> level
        cols = length // 8

        def get(q, level=level, cols=cols):
            if level == 0:
                return pad_ref[pl.ds(q, 8, stride=cols), :]
            return level_ref[level - 1, q]

        window = [get(q) for q in range(LAGMAX)]
        products = [None] * LAGMAX
        total = None
        heads = []
        tails = [None] * LAGMAX
        previous = None
        for q in range(cols):
            window.append(get(q + LAGMAX))
            base = window[q]
            total = base if total is None else total + base
            if q < LAGMAX:
                heads.append(base[0:1])
            if q >= cols - LAGMAX:
                tails[cols - 1 - q] = base[7:8]
            for d in range(1, LAGMAX + 1):
                term = base * window[q + d]
                products[d - 1] = term if products[d - 1] is None else products[d - 1] + term
            if level + 1 < LEVELS:
                if q % 2 == 0:
                    previous = base
                else:
                    mean = (previous + base) * 0.5
                    level_ref[level, q // 2] = mean
                    if q // 2 < LAGMAX:
                        halo = jnp.where(sub < 7, pltpu.roll(mean, 7, 0), 0.0)
                        level_ref[level, cols // 2 + q // 2] = halo
        whole = jnp.sum(total, 0, keepdims=True)
        first, second = whole, whole
        for d in range(1, LAGMAX + 1):
            first = first - tails[d - 1]
            second = second - heads[d - 1]
            product = jnp.sum(products[d - 1], 0, keepdims=True)
            denom = first * second
            safe = jnp.where(denom > 0, denom, 1.0)
            value = jnp.where(denom > 0, product * float(length - d) / safe, 0.0)
            table_ref[level * LAGMAX + d - 1, pl.ds(b, 1), :] = value


def far_first(ny, nx):
    offsets = [(dy, dx, dc) for dy in range(ny) for dx in range(nx) for dc in range(2)][1:]
    return sorted(offsets, key=lambda o: -(min(o[0], ny - o[0]) + min(o[1], nx - o[1])))


def core(
    ntm,
    nrows,
    lag_ref,
    owner_ref,
    slot_ref,
    frames_ref,
    g2_ref,
    two_ref,
    raw,
    flat,
    near_out,
    wide_out,
    wide_in,
    near_in,
    table_vec,
    table,
    pad_ref,
    level_ref,
    corr_ref,
    gram_ref,
    sums_ref,
    tall_ref,
    out_buf,
    in_buf,
    local_sem,
    wide_send,
    wide_recv,
    near_send,
    near_recv,
    sum_send,
    sum_recv,
    ring_send,
    ring_recv,
):
    me = lax.axis_index("tm")
    row = lax.axis_index("rows")
    nx = 4
    ny = ntm // (2 * nx)
    barrier = pltpu.get_barrier_semaphore()
    load = pltpu.make_async_copy(frames_ref.at[:, 0], raw, local_sem.at[0])
    load.start()

    def hello_tm(i, carry):
        peer = lax.rem(me + i, ntm)
        pl.semaphore_signal(barrier, inc=1, device_id=(peer, row), device_id_type=MESH)
        return carry

    def hello_rows(i, carry):
        peer = lax.rem(row + i, nrows)
        pl.semaphore_signal(barrier, inc=1, device_id=(me, peer), device_id_type=MESH)
        return carry

    lax.fori_loop(1, ntm, hello_tm, 0)
    lax.fori_loop(1, nrows, hello_rows, 0)

    span, nblocks, width = raw.shape
    halves, _, half = wide_in.shape[:3]
    slots = halves * half
    pitch = 16
    near = near_in.shape[1]
    square = (nblocks, nblocks)
    owners = owner_ref[pl.ds(row, 1), :].astype(jnp.float32)
    cycles = slot_ref[pl.ds(row, 1), :].astype(jnp.float32)
    down = lax.broadcasted_iota(jnp.int32, square, 0)
    along = lax.broadcasted_iota(jnp.int32, square, 1)
    alongf = along.astype(jnp.float32)
    across = jnp.broadcast_to(owners, square)
    same = (across == across.T) & (down < along)
    rank = jnp.sum(jnp.where(same, 1.0, 0.0), 0, keepdims=True)
    place = jnp.broadcast_to(owners * float(pitch) + rank, square).T
    entry = jnp.broadcast_to(alongf[0:1] + float(nblocks) * (1.0 + cycles), square).T
    parts = ntm * pitch // nblocks
    rows_of = [
        jnp.sum(jnp.where(place == alongf + float(j * nblocks), entry, 0.0), 0, keepdims=True)
        for j in range(parts)
    ]
    table_vec[...] = jnp.concatenate(
        rows_of + [jnp.zeros((8 - parts, nblocks), jnp.float32)], 0
    ).astype(jnp.int32)
    fetch = pltpu.make_async_copy(table_vec, table, local_sem.at[1])
    fetch.start()
    pad_ref[...] = jnp.zeros_like(pad_ref)
    load.wait()
    flat[...] = raw[...].astype(jnp.float32).reshape(span * nblocks, width)

    def turn(b, carry):
        near_out[b] = flat[pl.ds(b, span, stride=nblocks), :].astype(jnp.bfloat16)
        return carry

    lax.fori_loop(0, nblocks, turn, 0, unroll=8)
    fetch.wait()

    per = nblocks // pitch

    def entry_at(owner, k):
        return table[owner // per, (owner % per) * pitch + k]

    def fill(o, carry):
        tiles = [near_out[entry_at(o, k) & (nblocks - 1)] for k in range(slots)]
        for k in range(slots):
            wide_out[k // half, o, k % half] = tiles[k]
        return carry

    lax.fori_loop(0, ntm, fill, 0)
    for h in range(halves):
        wide_in[h, me] = wide_out[h, me]
    near_in[me] = near_out[pl.ds(pl.multiple_of(me * near, near), near)]
    pl.semaphore_wait(barrier, ntm + nrows - 2)

    order = far_first(ny, nx)
    y, x, c = me // (2 * nx), (me // 2) % nx, me % 2

    def peer_at(offset):
        dy, dx, dc = offset
        return (lax.rem(y + dy, ny) * nx + lax.rem(x + dx, nx)) * 2 + lax.rem(c + dc, 2)

    def wide_copy(h, peer):
        return pltpu.make_async_remote_copy(
            src_ref=wide_out.at[h, peer],
            dst_ref=wide_in.at[h, me],
            send_sem=wide_send.at[h, peer],
            recv_sem=wide_recv.at[h, me],
            device_id=(peer, row),
            device_id_type=MESH,
        )

    def near_copy(peer):
        return pltpu.make_async_remote_copy(
            src_ref=near_out.at[pl.ds(pl.multiple_of(peer * near, near), near)],
            dst_ref=near_in.at[me],
            send_sem=near_send.at[peer],
            recv_sem=near_recv.at[me],
            device_id=(peer, row),
            device_id_type=MESH,
        )

    def arrival(ref, sem, peer):
        return pltpu.make_async_remote_copy(
            src_ref=ref,
            dst_ref=ref,
            send_sem=sem,
            recv_sem=sem,
            device_id=(peer, row),
            device_id_type=MESH,
        )

    def wide_arrival(h, peer):
        return arrival(wide_in.at[h, peer], wide_recv.at[h, peer], peer)

    def each(body):
        def step(i, carry):
            body(lax.rem(me + i, ntm))
            return carry

        lax.fori_loop(1, ntm, step, 0)

    def sum_copy(i):
        peer = lax.rem(row + i, nrows)
        return pltpu.make_async_remote_copy(
            src_ref=sums_ref.at[row],
            dst_ref=sums_ref.at[row],
            send_sem=sum_send.at[i],
            recv_sem=sum_recv.at[row],
            device_id=(me, peer),
            device_id_type=MESH,
        )

    def sum_arrival(i):
        peer = lax.rem(row + i, nrows)
        return pltpu.make_async_remote_copy(
            src_ref=sums_ref.at[peer],
            dst_ref=sums_ref.at[peer],
            send_sem=sum_recv.at[peer],
            recv_sem=sum_recv.at[peer],
            device_id=(me, peer),
            device_id_type=MESH,
        )

    for h in range(halves):
        for offset in order:
            wide_copy(h, peer_at(offset)).start()
    for offset in order:
        near_copy(peer_at(offset)).start()

    nf = ntm * span
    slab_len = nf // nrows
    contract = (((1,), (1,)), ((), ()))
    own_entries = [entry_at(me, k) // nblocks for k in range(slots)]
    sums_own = None
    for h in range(halves):
        lines = [
            jnp.concatenate(
                [
                    jnp.full((1, width), jnp.where(e == a + 1, 1.0, 0.0), jnp.float32)
                    for e in own_entries[h * half : (h + 1) * half]
                ],
                1,
            )
            for a in range(2)
        ]
        masks = jnp.concatenate(lines + [jnp.zeros((6, half * width), jnp.float32)], 0)
        masks = masks.astype(jnp.bfloat16)
        each(lambda peer: wide_arrival(h, peer).wait_recv())
        pixels = jnp.concatenate([wide_in[h, :, k].reshape(nf, width) for k in range(half)], 1)
        term = lax.dot_general(masks, pixels, contract, preferred_element_type=jnp.float32)
        sums_own = term if sums_own is None else sums_own + term
        if h + 1 == halves:
            sums_own = sums_own[0:2]
            sums_ref[row] = sums_own
            for i in range(1, nrows):
                sum_copy(i).start()
        for a in range(2):
            part = lax.dot_general(
                pixels * masks[a : a + 1, :], pixels, contract, preferred_element_type=jnp.float32
            )
            if h:
                gram_ref[a] += part
            else:
                gram_ref[a] = part

    cycle_all = owner_ref[...] * 2 + slot_ref[...]
    group = lax.broadcasted_iota(jnp.int32, (nrows, 1), 0)
    behind = lax.rem(row - group + nrows, nrows)
    ahead = lax.rem(group - row + nrows, nrows)
    pixel_counts = [
        jnp.sum(jnp.where(cycle_all == me * 2 + a, float(width), 0.0), 1, keepdims=True) for a in range(2)
    ]

    def count_of(a, inside):
        return jnp.sum(jnp.where(inside, pixel_counts[a], 0.0), 0, keepdims=True)

    def inverse(v):
        return jnp.where(v > 0, 1.0 / jnp.where(v > 0, v, 1.0), 0.0)

    def sums_at(i):
        return sums_ref[lax.rem(row + i, nrows)]

    def tall_at(slab, lane):
        start = pl.multiple_of(slab * slab_len, slab_len)
        return tall_ref[pl.ds(start, slab_len), lane : lane + 1]

    def own_part(a, slab):
        start = pl.multiple_of(slab * slab_len, slab_len)
        return gram_ref[a, pl.ds(start, slab_len), :]

    def ring_copy(flow, step):
        _, way, hops = FLOWS[flow]
        return pltpu.make_async_remote_copy(
            src_ref=out_buf.at[flow, step],
            dst_ref=in_buf.at[flow, step],
            send_sem=ring_send.at[flow, step],
            recv_sem=ring_recv.at[flow, step],
            device_id=(me, lax.rem(row + way + nrows, nrows)),
            device_id_type=MESH,
        )

    def tau(b, carry):
        multitau_block(b, near_in, pad_ref, level_ref, corr_ref)
        return carry

    def decode(flow, step, slab, lane, line):
        a, way, _ = FLOWS[flow]
        distance = behind if way > 0 else ahead
        count = count_of(a, (distance >= 1) & (distance <= step))
        value = (in_buf[flow, step - 1].astype(jnp.int32) + BIAS).astype(jnp.float32)
        return value * (tall_at(slab, lane) * (inverse(count) * (1.0 / CODE))) * line

    up = jnp.zeros_like(sums_own)
    dn = jnp.zeros_like(sums_own)
    for step in range(STEPS):
        if step:
            sum_arrival(step).wait_recv()
            sum_arrival(nrows - step).wait_recv()
            up = up + sums_at(nrows - step)
            dn = dn + sums_at(step)
        lines = jnp.concatenate([up, dn, inverse(up + sums_own), inverse(dn + sums_own)], 0)
        tall_ref[...] = lines.T
        for flow, (a, way, hops) in enumerate(FLOWS):
            if step >= hops:
                continue
            slab = lax.rem(row + way * (hops - step) + nrows, nrows)
            lane = a if way > 0 else 2 + a
            value = own_part(a, slab)
            if step:
                ring_copy(flow, step - 1).wait_recv()
                value = value + decode(flow, step, slab, lane, lines[lane : lane + 1])
            count = count_of(a, (behind if way > 0 else ahead) <= step)
            scale = tall_at(slab, lane + 4) * (count * CODE)
            code = (value * scale * lines[lane + 4 : lane + 5] + 0.5).astype(jnp.int32) - BIAS
            out_buf[flow, step] = code.astype(jnp.int16)
            ring_copy(flow, step).start()
        if step == 2:
            each(lambda peer: arrival(near_in.at[peer], near_recv.at[peer], peer).wait_recv())
        if step >= 2:
            lax.fori_loop(2 * step - 4, 2 * step - 2, tau, 0)

    for l in range(LEVELS):
        for j in range(lag_ref.shape[1]):
            g2_ref[l * lag_ref.shape[1] + j] = corr_ref[
                l * LAGMAX + jnp.maximum(lag_ref[l, j] - 1, 0)
            ]
    sum_arrival(STEPS).wait_recv()
    last = sums_at(STEPS)
    sums = sums_own + up + dn + last
    ends = [up[0:1] + last[0:1], up[1:2], dn[0:1], dn[1:2] + last[1:2]]
    lines = jnp.concatenate(ends + [sums, sums], 0)
    tall_ref[...] = lines.T
    total = [own_part(a, row) for a in range(2)]
    for flow, (a, way, hops) in enumerate(FLOWS):
        ring_copy(flow, hops - 1).wait_recv()
        lane = a if way > 0 else 2 + a
        total[a] = total[a] + decode(flow, hops, row, lane, lines[lane : lane + 1])
    for a in range(2):
        denom = jnp.maximum(tall_at(row, 4 + a) * sums[a : a + 1], 1.0)
        two_ref[:, a, :] = total[a] * (count_of(a, behind >= 0) / denom)

    for h in range(halves):
        each(lambda peer: wide_copy(h, peer).wait_send())
    each(lambda peer: near_copy(peer).wait_send())
    for i in range(1, nrows):
        sum_copy(i).wait_send()
    for flow, (a, way, hops) in enumerate(FLOWS):
        for step in range(hops):
            ring_copy(flow, step).wait_send()


def shards(frames, block_owner, cycle_slot, lag_table):
    span, _, nblocks, width = frames.shape
    ntm = lax.axis_size("tm")
    nrows = lax.axis_size("rows")
    cap = 3 * nblocks // ntm
    near = nblocks // ntm
    nf = span * ntm
    slab = nf // nrows
    nflow = len(FLOWS)
    vmem = pl.BlockSpec(memory_space=pltpu.VMEM)
    smem = pl.BlockSpec(memory_space=pltpu.SMEM)
    dma = pltpu.SemaphoreType.DMA
    bf16, f32, i32, i16 = jnp.bfloat16, jnp.float32, jnp.int32, jnp.int16
    g2, two = pl.pallas_call(
        functools.partial(core, ntm, nrows),
        out_shape=(
            jax.ShapeDtypeStruct((LEVELS * lag_table.shape[1], near, width), f32),
            jax.ShapeDtypeStruct((slab, 2, nf), f32),
        ),
        in_specs=[smem, vmem, vmem, pl.BlockSpec(memory_space=pl.ANY)],
        out_specs=(vmem, vmem),
        scratch_shapes=[
            pltpu.VMEM((span, nblocks, width), bf16),
            pltpu.VMEM((span * nblocks, width), f32),
            pltpu.VMEM((nblocks, span, width), bf16),
            pltpu.VMEM((2, ntm, cap // 2, span, width), bf16),
            pltpu.VMEM((2, ntm, cap // 2, span, width), bf16),
            pltpu.VMEM((ntm, near, span, width), bf16),
            pltpu.VMEM((8, nblocks), i32),
            pltpu.SMEM((8, nblocks), i32),
            pltpu.VMEM((nf + 64, width), f32),
            pltpu.VMEM((LEVELS - 1, nf // 16 + LAGMAX, 8, width), f32),
            pltpu.VMEM((LEVELS * LAGMAX, near, width), f32),
            pltpu.VMEM((2, nf, nf), f32),
            pltpu.VMEM((nrows, 2, nf), f32),
            pltpu.VMEM((nf, 8), f32),
            pltpu.VMEM((nflow, STEPS, slab, nf), i16),
            pltpu.VMEM((nflow, STEPS, slab, nf), i16),
            dma((2,)),
            dma((2, ntm)),
            dma((2, ntm)),
            dma((ntm,)),
            dma((ntm,)),
            dma((nrows,)),
            dma((nrows,)),
            dma((nflow, STEPS)),
            dma((nflow, STEPS)),
        ],
        compiler_params=pltpu.CompilerParams(collective_id=0, has_side_effects=True),
    )(lag_table, block_owner[:, :, 0], cycle_slot, frames)
    return g2[None], two


def solution(mesh):
    in_specs = (P("tm", "rows", None, None), P(), P(), P())
    out_specs = (P("rows", None, "tm", None), P("rows", "tm", None))
    return jax.shard_map(shards, mesh=mesh, in_specs=in_specs, out_specs=out_specs, check_vma=False)
```

```python
import functools

import jax
import jax.numpy as jnp
from jax import lax
from jax.experimental import pallas as pl
from jax.experimental.pallas import tpu as pltpu
from jax.sharding import PartitionSpec as P

CYCLES = 64
LEVELS = 4
LAGMAX = 8
MESH = pl.DeviceIdType.MESH
FLOWS = ((0, 1, 4), (1, -1, 4), (0, -1, 3), (1, 1, 3))
STEPS = 4
CODE = 14500.0
BIAS = 32767


def multitau_block(b, recv_ref, pad_ref, level_ref, table_ref):
    nf = recv_ref.shape[0] * recv_ref.shape[2]
    width = recv_ref.shape[3]
    pad_ref[pl.ds(0, nf), :] = recv_ref[:, b].astype(jnp.float32).reshape(nf, width)
    sub = lax.broadcasted_iota(jnp.int32, (8, width), 0)
    for level in range(LEVELS):
        length = nf >> level
        cols = length // 8

        def get(q, level=level, cols=cols):
            if level == 0:
                return pad_ref[pl.ds(q, 8, stride=cols), :]
            return level_ref[level - 1, q]

        window = [get(q) for q in range(LAGMAX)]
        products = [None] * LAGMAX
        total = None
        heads = []
        tails = [None] * LAGMAX
        previous = None
        for q in range(cols):
            window.append(get(q + LAGMAX))
            base = window[q]
            total = base if total is None else total + base
            if q < LAGMAX:
                heads.append(base[0:1])
            if q >= cols - LAGMAX:
                tails[cols - 1 - q] = base[7:8]
            for d in range(1, LAGMAX + 1):
                term = base * window[q + d]
                products[d - 1] = term if products[d - 1] is None else products[d - 1] + term
            if level + 1 < LEVELS:
                if q % 2 == 0:
                    previous = base
                else:
                    mean = (previous + base) * 0.5
                    level_ref[level, q // 2] = mean
                    if q // 2 < LAGMAX:
                        halo = jnp.where(sub < 7, pltpu.roll(mean, 7, 0), 0.0)
                        level_ref[level, cols // 2 + q // 2] = halo
        whole = jnp.sum(total, 0, keepdims=True)
        first, second = whole, whole
        for d in range(1, LAGMAX + 1):
            first = first - tails[d - 1]
            second = second - heads[d - 1]
            product = jnp.sum(products[d - 1], 0, keepdims=True)
            denom = first * second
            safe = jnp.where(denom > 0, denom, 1.0)
            value = jnp.where(denom > 0, product * float(length - d) / safe, 0.0)
            table_ref[level * LAGMAX + d - 1, pl.ds(b, 1), :] = value


def far_first(ny, nx):
    offsets = [(dy, dx, dc) for dy in range(ny) for dx in range(nx) for dc in range(2)][1:]
    order = []
    for dy, dx, dc in sorted(offsets, key=lambda o: -(min(o[0], ny - o[0]) + min(o[1], nx - o[1]))):
        for offset in ((dy, dx, dc), (-dy % ny, -dx % nx, dc)):
            if offset not in order:
                order.append(offset)
    return order


def core(
    ntm,
    nrows,
    lag_ref,
    owner_ref,
    slot_ref,
    frames_ref,
    g2_ref,
    two_ref,
    raw,
    flat,
    near_out,
    wide_out,
    wide_in,
    near_in,
    table_vec,
    table,
    pad_ref,
    level_ref,
    corr_ref,
    gram_ref,
    sums_ref,
    tall_ref,
    out_buf,
    in_buf,
    local_sem,
    wide_send,
    wide_recv,
    near_send,
    near_recv,
    sum_send,
    sum_recv,
    ring_send,
    ring_recv,
):
    me = lax.axis_index("tm")
    row = lax.axis_index("rows")
    nx = 4
    ny = ntm // (2 * nx)
    barrier = pltpu.get_barrier_semaphore()
    load = pltpu.make_async_copy(frames_ref.at[:, 0], raw, local_sem.at[0])
    load.start()

    for i in range(1, ntm):
        peer = lax.rem(me + i, ntm)
        pl.semaphore_signal(barrier, inc=1, device_id=(peer, row), device_id_type=MESH)
    for i in range(1, nrows):
        peer = lax.rem(row + i, nrows)
        pl.semaphore_signal(barrier, inc=1, device_id=(me, peer), device_id_type=MESH)

    span, nblocks, width = raw.shape
    halves, _, half = wide_in.shape[:3]
    slots = halves * half
    pitch = 16
    near = near_in.shape[1]
    square = (nblocks, nblocks)
    owners = owner_ref[pl.ds(row, 1), :].astype(jnp.float32)
    cycles = slot_ref[pl.ds(row, 1), :].astype(jnp.float32)
    down = lax.broadcasted_iota(jnp.int32, square, 0)
    along = lax.broadcasted_iota(jnp.int32, square, 1)
    alongf = along.astype(jnp.float32)
    across = jnp.broadcast_to(owners, square)
    same = (across == across.T) & (down < along)
    rank = jnp.sum(jnp.where(same, 1.0, 0.0), 0, keepdims=True)
    place = jnp.broadcast_to(owners * float(pitch) + rank, square).T
    entry = jnp.broadcast_to(alongf[0:1] + float(nblocks) * (1.0 + cycles), square).T
    parts = ntm * pitch // nblocks
    rows_of = [
        jnp.sum(jnp.where(place == alongf + float(j * nblocks), entry, 0.0), 0, keepdims=True)
        for j in range(parts)
    ]
    table_vec[...] = jnp.concatenate(
        rows_of + [jnp.zeros((8 - parts, nblocks), jnp.float32)], 0
    ).astype(jnp.int32)
    fetch = pltpu.make_async_copy(table_vec, table, local_sem.at[1])
    fetch.start()
    pad_ref[...] = jnp.zeros_like(pad_ref)
    load.wait()
    flat[...] = raw[...].astype(jnp.float32).reshape(span * nblocks, width)

    def turn(b, carry):
        near_out[b] = flat[pl.ds(b, span, stride=nblocks), :].astype(jnp.bfloat16)
        return carry

    lax.fori_loop(0, nblocks, turn, 0, unroll=8)
    fetch.wait()

    per = nblocks // pitch

    def entry_at(owner, k):
        return table[owner // per, (owner % per) * pitch + k]

    def fill(h):
        def place_owner(o, carry):
            tiles = [near_out[entry_at(o, h * half + k) & (nblocks - 1)] for k in range(half)]
            for k in range(half):
                wide_out[h, o, k] = tiles[k]
            return carry

        lax.fori_loop(0, ntm, place_owner, 0, unroll=2)
        wide_in[h, me] = wide_out[h, me]

    fill(0)
    near_in[me] = near_out[pl.ds(pl.multiple_of(me * near, near), near)]
    pl.semaphore_wait(barrier, ntm + nrows - 2)

    order = far_first(ny, nx)
    y, x, c = me // (2 * nx), (me // 2) % nx, me % 2

    def peer_at(offset):
        dy, dx, dc = offset
        return (lax.rem(y + dy, ny) * nx + lax.rem(x + dx, nx)) * 2 + lax.rem(c + dc, 2)

    def wide_copy(h, peer):
        return pltpu.make_async_remote_copy(
            src_ref=wide_out.at[h, peer],
            dst_ref=wide_in.at[h, me],
            send_sem=wide_send.at[h],
            recv_sem=wide_recv.at[h],
            device_id=(peer, row),
            device_id_type=MESH,
        )

    def near_copy(peer):
        return pltpu.make_async_remote_copy(
            src_ref=near_out.at[pl.ds(pl.multiple_of(peer * near, near), near)],
            dst_ref=near_in.at[me],
            send_sem=near_send.at[0],
            recv_sem=near_recv.at[0],
            device_id=(peer, row),
            device_id_type=MESH,
        )

    def batch(ref, send, recv):
        return pltpu.make_async_remote_copy(
            src_ref=ref.at[pl.ds(0, ntm - 1)],
            dst_ref=ref.at[pl.ds(0, ntm - 1)],
            send_sem=send,
            recv_sem=recv,
            device_id=(lax.rem(me + 1, ntm), row),
            device_id_type=MESH,
        )

    def wide_batch(h):
        return batch(wide_in.at[h], wide_send.at[h], wide_recv.at[h])

    near_batch = batch(near_in, near_send.at[0], near_recv.at[0])

    def sum_copy(i):
        peer = lax.rem(row + i, nrows)
        return pltpu.make_async_remote_copy(
            src_ref=sums_ref.at[row],
            dst_ref=sums_ref.at[row],
            send_sem=sum_send.at[i],
            recv_sem=sum_recv.at[row],
            device_id=(me, peer),
            device_id_type=MESH,
        )

    def sum_arrival(i):
        peer = lax.rem(row + i, nrows)
        return pltpu.make_async_remote_copy(
            src_ref=sums_ref.at[peer],
            dst_ref=sums_ref.at[peer],
            send_sem=sum_recv.at[peer],
            recv_sem=sum_recv.at[peer],
            device_id=(me, peer),
            device_id_type=MESH,
        )

    peers = [peer_at(offset) for offset in order]
    for h in range(halves):
        if h:
            fill(h)
        for peer in peers:
            wide_copy(h, peer).start()
    for peer in peers:
        near_copy(peer).start()

    nf = ntm * span
    slab_len = nf // nrows
    contract = (((1,), (1,)), ((), ()))
    own_entries = [entry_at(me, k) // nblocks for k in range(slots)]
    sums_own = None
    for h in range(halves):
        lines = [
            jnp.concatenate(
                [
                    jnp.full((1, width), jnp.where(e == a + 1, 1.0, 0.0), jnp.float32)
                    for e in own_entries[h * half : (h + 1) * half]
                ],
                1,
            )
            for a in range(2)
        ]
        masks = jnp.concatenate(lines + [jnp.zeros((14, half * width), jnp.float32)], 0)
        masks = masks.astype(jnp.bfloat16)
        wide_batch(h).wait_recv()
        pixels = jnp.concatenate([wide_in[h, :, k].reshape(nf, width) for k in range(half)], 1)
        left = jnp.concatenate([pixels * masks[0:1], pixels * masks[1:2], masks], 0)
        part = lax.dot_general(left, pixels, contract, preferred_element_type=jnp.float32)
        for a in range(2):
            term = part[a * nf : (a + 1) * nf]
            if h:
                gram_ref[a] += term
            else:
                gram_ref[a] = term
        term = part[2 * nf : 2 * nf + 2]
        sums_own = sums_own + term if h else term
    sums_ref[row] = sums_own
    for i in range(1, nrows):
        sum_copy(i).start()

    cycle_all = owner_ref[...] * 2 + slot_ref[...]
    group = lax.broadcasted_iota(jnp.int32, (nrows, 1), 0)
    behind = lax.rem(row - group + nrows, nrows)
    ahead = lax.rem(group - row + nrows, nrows)
    pixel_counts = [
        jnp.sum(jnp.where(cycle_all == me * 2 + a, float(width), 0.0), 1, keepdims=True) for a in range(2)
    ]

    def count_of(a, inside):
        return jnp.sum(jnp.where(inside, pixel_counts[a], 0.0), 0, keepdims=True)

    def inverse(v):
        return jnp.where(v > 0, 1.0 / jnp.where(v > 0, v, 1.0), 0.0)

    def sums_at(i):
        return sums_ref[lax.rem(row + i, nrows)]

    def tall_at(slab, lane):
        start = pl.multiple_of(slab * slab_len, slab_len)
        return tall_ref[pl.ds(start, slab_len), lane : lane + 1]

    def own_part(a, slab):
        start = pl.multiple_of(slab * slab_len, slab_len)
        return gram_ref[a, pl.ds(start, slab_len), :]

    def ring_copy(flow, step):
        _, way, hops = FLOWS[flow]
        return pltpu.make_async_remote_copy(
            src_ref=out_buf.at[flow, step],
            dst_ref=in_buf.at[flow, step],
            send_sem=ring_send.at[flow, step],
            recv_sem=ring_recv.at[flow, step],
            device_id=(me, lax.rem(row + way + nrows, nrows)),
            device_id_type=MESH,
        )

    def tau(b, carry):
        multitau_block(b, near_in, pad_ref, level_ref, corr_ref)
        return carry

    def decode(flow, step, slab, lane, line):
        a, way, _ = FLOWS[flow]
        distance = behind if way > 0 else ahead
        count = count_of(a, (distance >= 1) & (distance <= step))
        value = (in_buf[flow, step - 1].astype(jnp.int32) + BIAS).astype(jnp.float32)
        return value * (tall_at(slab, lane) * (inverse(count) * (1.0 / CODE))) * line

    up = jnp.zeros_like(sums_own)
    dn = jnp.zeros_like(sums_own)
    for step in range(STEPS):
        if step:
            sum_arrival(step).wait_recv()
            sum_arrival(nrows - step).wait_recv()
            up = up + sums_at(nrows - step)
            dn = dn + sums_at(step)
        lines = jnp.concatenate([up, dn, inverse(up + sums_own), inverse(dn + sums_own)], 0)
        tall_ref[...] = lines.T
        for flow, (a, way, hops) in enumerate(FLOWS):
            if step >= hops:
                continue
            slab = lax.rem(row + way * (hops - step) + nrows, nrows)
            lane = a if way > 0 else 2 + a
            value = own_part(a, slab)
            if step:
                ring_copy(flow, step - 1).wait_recv()
                value = value + decode(flow, step, slab, lane, lines[lane : lane + 1])
            count = count_of(a, (behind if way > 0 else ahead) <= step)
            scale = tall_at(slab, lane + 4) * (count * CODE)
            code = (value * scale * lines[lane + 4 : lane + 5] + 0.5).astype(jnp.int32) - BIAS
            out_buf[flow, step] = code.astype(jnp.int16)
            ring_copy(flow, step).start()
    near_batch.wait_recv()
    lax.fori_loop(0, near, tau, 0)

    for l in range(LEVELS):
        for j in range(lag_ref.shape[1]):
            g2_ref[l * lag_ref.shape[1] + j] = corr_ref[
                l * LAGMAX + jnp.maximum(lag_ref[l, j] - 1, 0)
            ]
    sum_arrival(STEPS).wait_recv()
    last = sums_at(STEPS)
    sums = sums_own + up + dn + last
    ends = [up[0:1] + last[0:1], up[1:2], dn[0:1], dn[1:2] + last[1:2]]
    lines = jnp.concatenate(ends + [sums, sums], 0)
    tall_ref[...] = lines.T
    total = [own_part(a, row) for a in range(2)]
    for flow, (a, way, hops) in enumerate(FLOWS):
        ring_copy(flow, hops - 1).wait_recv()
        lane = a if way > 0 else 2 + a
        total[a] = total[a] + decode(flow, hops, row, lane, lines[lane : lane + 1])
    for a in range(2):
        denom = jnp.maximum(tall_at(row, 4 + a) * sums[a : a + 1], 1.0)
        two_ref[:, a, :] = total[a] * (count_of(a, behind >= 0) / denom)

    for h in range(halves):
        wide_batch(h).wait_send()
    near_batch.wait_send()
    for i in range(1, nrows):
        sum_copy(i).wait_send()
    for flow, (a, way, hops) in enumerate(FLOWS):
        for step in range(hops):
            ring_copy(flow, step).wait_send()


def finish(g2_ref, two_ref, g2_out, two_out, sem):
    first = pltpu.make_async_copy(g2_ref, g2_out, sem.at[0])
    second = pltpu.make_async_copy(two_ref, two_out, sem.at[1])
    first.start()
    second.start()
    first.wait()
    second.wait()


def shards(frames, block_owner, cycle_slot, lag_table):
    span, _, nblocks, width = frames.shape
    ntm = lax.axis_size("tm")
    nrows = lax.axis_size("rows")
    cap = 3 * nblocks // ntm
    near = nblocks // ntm
    nf = span * ntm
    slab = nf // nrows
    nflow = len(FLOWS)
    vmem = pl.BlockSpec(memory_space=pltpu.VMEM)
    smem = pl.BlockSpec(memory_space=pltpu.SMEM)
    dma = pltpu.SemaphoreType.DMA
    bf16, f32, i32, i16 = jnp.bfloat16, jnp.float32, jnp.int32, jnp.int16
    g2, two = pl.pallas_call(
        functools.partial(core, ntm, nrows),
        out_shape=(
            pltpu.VMEM((LEVELS * lag_table.shape[1], near, width), f32),
            pltpu.VMEM((slab, 2, nf), f32),
        ),
        in_specs=[smem, vmem, vmem, pl.BlockSpec(memory_space=pl.ANY)],
        out_specs=(vmem, vmem),
        scratch_shapes=[
            pltpu.VMEM((span, nblocks, width), bf16),
            pltpu.VMEM((span * nblocks, width), f32),
            pltpu.VMEM((nblocks, span, width), bf16),
            pltpu.VMEM((2, ntm, cap // 2, span, width), bf16),
            pltpu.VMEM((2, ntm, cap // 2, span, width), bf16),
            pltpu.VMEM((ntm, near, span, width), bf16),
            pltpu.VMEM((8, nblocks), i32),
            pltpu.SMEM((8, nblocks), i32),
            pltpu.VMEM((nf + 64, width), f32),
            pltpu.VMEM((LEVELS - 1, nf // 16 + LAGMAX, 8, width), f32),
            pltpu.VMEM((LEVELS * LAGMAX, near, width), f32),
            pltpu.VMEM((2, nf, nf), f32),
            pltpu.VMEM((nrows, 2, nf), f32),
            pltpu.VMEM((nf, 8), f32),
            pltpu.VMEM((nflow, STEPS, slab, nf), i16),
            pltpu.VMEM((nflow, STEPS, slab, nf), i16),
            dma((2,)),
            dma((2,)),
            dma((2,)),
            dma((1,)),
            dma((1,)),
            dma((nrows,)),
            dma((nrows,)),
            dma((nflow, STEPS)),
            dma((nflow, STEPS)),
        ],
        compiler_params=pltpu.CompilerParams(collective_id=0, has_side_effects=True),
    )(lag_table, block_owner[:, :, 0], cycle_slot, frames)
    g2 = pltpu.with_memory_space_constraint(g2, pltpu.VMEM)
    two = pltpu.with_memory_space_constraint(two, pltpu.VMEM)
    hbm = pl.BlockSpec(memory_space=pl.ANY)
    g2, two = pl.pallas_call(
        finish,
        out_shape=(jax.ShapeDtypeStruct(g2.shape, f32), jax.ShapeDtypeStruct(two.shape, f32)),
        in_specs=[vmem, vmem],
        out_specs=(hbm, hbm),
        scratch_shapes=[dma((2,))],
    )(g2, two)
    return g2[None], two


def solution(mesh):
    in_specs = (P("tm", "rows", None, None), P(), P(), P())
    out_specs = (P("rows", None, "tm", None), P("rows", "tm", None))
    return jax.shard_map(shards, mesh=mesh, in_specs=in_specs, out_specs=out_specs, check_vma=False)
```

```python
import functools

import jax
import jax.numpy as jnp
from jax import lax
from jax.experimental import pallas as pl
from jax.experimental.pallas import tpu as pltpu
from jax.sharding import PartitionSpec as P

CYCLES = 64
LEVELS = 4
LAGMAX = 8
MESH = pl.DeviceIdType.MESH
PIECES = 1
CHAINS = ((0, 1, 4), (1, -1, 4), (0, -1, 3), (1, 1, 3))
FLOWS = tuple((a, way, hops, piece) for piece in range(PIECES) for a, way, hops in CHAINS)
STEPS = 4
CODE = 14500.0
BIAS = 32767


def multitau_block(b, recv_ref, pad_ref, level_ref, table_ref):
    nf = recv_ref.shape[0] * recv_ref.shape[2]
    width = recv_ref.shape[3]
    pad_ref[pl.ds(0, nf), :] = recv_ref[:, b].astype(jnp.float32).reshape(nf, width)
    sub = lax.broadcasted_iota(jnp.int32, (8, width), 0)
    for level in range(LEVELS):
        length = nf >> level
        cols = length // 8

        def get(q, level=level, cols=cols):
            if level == 0:
                return pad_ref[pl.ds(q, 8, stride=cols), :]
            return level_ref[level - 1, q]

        window = [get(q) for q in range(LAGMAX)]
        products = [None] * LAGMAX
        total = None
        heads = []
        tails = [None] * LAGMAX
        previous = None
        for q in range(cols):
            window.append(get(q + LAGMAX))
            base = window[q]
            total = base if total is None else total + base
            if q < LAGMAX:
                heads.append(base[0:1])
            if q >= cols - LAGMAX:
                tails[cols - 1 - q] = base[7:8]
            for d in range(1, LAGMAX + 1):
                term = base * window[q + d]
                products[d - 1] = term if products[d - 1] is None else products[d - 1] + term
            if level + 1 < LEVELS:
                if q % 2 == 0:
                    previous = base
                else:
                    mean = (previous + base) * 0.5
                    level_ref[level, q // 2] = mean
                    if q // 2 < LAGMAX:
                        halo = jnp.where(sub < 7, pltpu.roll(mean, 7, 0), 0.0)
                        level_ref[level, cols // 2 + q // 2] = halo
        whole = jnp.sum(total, 0, keepdims=True)
        first, second = whole, whole
        for d in range(1, LAGMAX + 1):
            first = first - tails[d - 1]
            second = second - heads[d - 1]
            product = jnp.sum(products[d - 1], 0, keepdims=True)
            denom = first * second
            safe = jnp.where(denom > 0, denom, 1.0)
            value = jnp.where(denom > 0, product * float(length - d) / safe, 0.0)
            table_ref[level * LAGMAX + d - 1, pl.ds(b, 1), :] = value


def far_first(ny, nx):
    offsets = [(dy, dx, dc) for dy in range(ny) for dx in range(nx) for dc in range(2)][1:]
    order = []
    for dy, dx, dc in sorted(offsets, key=lambda o: -(min(o[0], ny - o[0]) + min(o[1], nx - o[1]))):
        for offset in ((dy, dx, dc), (-dy % ny, -dx % nx, dc)):
            if offset not in order:
                order.append(offset)
    return order


def core(
    ntm,
    nrows,
    lag_ref,
    owner_ref,
    slot_ref,
    frames_ref,
    g2_ref,
    two_ref,
    raw,
    flat,
    near_out,
    wide_out,
    wide_in,
    near_in,
    table_vec,
    table,
    pad_ref,
    level_ref,
    corr_ref,
    gram_ref,
    sums_ref,
    tall_ref,
    count_ref,
    out_buf,
    in_buf,
    local_sem,
    wide_send,
    wide_recv,
    near_send,
    near_recv,
    sum_send,
    sum_recv,
    ring_send,
    ring_recv,
):
    me = lax.axis_index("tm")
    row = lax.axis_index("rows")
    nx = 4
    ny = ntm // (2 * nx)
    barrier = pltpu.get_barrier_semaphore()
    load = pltpu.make_async_copy(frames_ref.at[:, 0], raw, local_sem.at[0])
    load.start()

    for i in range(1, ntm):
        peer = lax.rem(me + i, ntm)
        pl.semaphore_signal(barrier, inc=1, device_id=(peer, row), device_id_type=MESH)
    for i in range(1, nrows):
        peer = lax.rem(row + i, nrows)
        pl.semaphore_signal(barrier, inc=1, device_id=(me, peer), device_id_type=MESH)

    span, nblocks, width = raw.shape
    halves, _, half = wide_in.shape[:3]
    slots = halves * half
    pitch = 16
    near = near_in.shape[1]
    square = (nblocks, nblocks)
    owners = owner_ref[pl.ds(row, 1), :].astype(jnp.float32)
    cycles = slot_ref[pl.ds(row, 1), :].astype(jnp.float32)
    down = lax.broadcasted_iota(jnp.int32, square, 0)
    along = lax.broadcasted_iota(jnp.int32, square, 1)
    alongf = along.astype(jnp.float32)
    across = jnp.broadcast_to(owners, square)
    same = (across == across.T) & (down < along)
    rank = jnp.sum(jnp.where(same, 1.0, 0.0), 0, keepdims=True)
    place = jnp.broadcast_to(owners * float(pitch) + rank, square).T
    entry = jnp.broadcast_to(alongf[0:1] + float(nblocks) * (1.0 + cycles), square).T
    parts = ntm * pitch // nblocks
    rows_of = [
        jnp.sum(jnp.where(place == alongf + float(j * nblocks), entry, 0.0), 0, keepdims=True)
        for j in range(parts)
    ]
    table_vec[...] = jnp.concatenate(
        rows_of + [jnp.zeros((8 - parts, nblocks), jnp.float32)], 0
    ).astype(jnp.int32)
    fetch = pltpu.make_async_copy(table_vec, table, local_sem.at[1])
    fetch.start()
    pad_ref[...] = jnp.zeros_like(pad_ref)
    load.wait()
    flat[...] = raw[...].astype(jnp.float32).reshape(span * nblocks, width)

    def turn(b, carry):
        near_out[b] = flat[pl.ds(b, span, stride=nblocks), :].astype(jnp.bfloat16)
        return carry

    lax.fori_loop(0, nblocks, turn, 0, unroll=8)
    fetch.wait()

    per = nblocks // pitch

    def entry_at(owner, k):
        return table[owner // per, (owner % per) * pitch + k]

    def fill(h):
        def place_owner(o, carry):
            tiles = [near_out[entry_at(o, h * half + k) & (nblocks - 1)] for k in range(half)]
            for k in range(half):
                wide_out[h, o, k] = tiles[k]
            return carry

        lax.fori_loop(0, ntm, place_owner, 0, unroll=2)
        wide_in[h, me] = wide_out[h, me]

    fill(0)
    near_in[me] = near_out[pl.ds(pl.multiple_of(me * near, near), near)]
    pl.semaphore_wait(barrier, ntm + nrows - 2)

    order = far_first(ny, nx)
    y, x, c = me // (2 * nx), (me // 2) % nx, me % 2

    def peer_at(offset):
        dy, dx, dc = offset
        return (lax.rem(y + dy, ny) * nx + lax.rem(x + dx, nx)) * 2 + lax.rem(c + dc, 2)

    def wide_copy(h, peer):
        return pltpu.make_async_remote_copy(
            src_ref=wide_out.at[h, peer],
            dst_ref=wide_in.at[h, me],
            send_sem=wide_send.at[h],
            recv_sem=wide_recv.at[h],
            device_id=(peer, row),
            device_id_type=MESH,
        )

    def near_copy(peer):
        return pltpu.make_async_remote_copy(
            src_ref=near_out.at[pl.ds(pl.multiple_of(peer * near, near), near)],
            dst_ref=near_in.at[me],
            send_sem=near_send.at[0],
            recv_sem=near_recv.at[0],
            device_id=(peer, row),
            device_id_type=MESH,
        )

    def batch(ref, send, recv):
        return pltpu.make_async_remote_copy(
            src_ref=ref.at[pl.ds(0, ntm - 1)],
            dst_ref=ref.at[pl.ds(0, ntm - 1)],
            send_sem=send,
            recv_sem=recv,
            device_id=(lax.rem(me + 1, ntm), row),
            device_id_type=MESH,
        )

    def wide_batch(h):
        return batch(wide_in.at[h], wide_send.at[h], wide_recv.at[h])

    near_batch = batch(near_in, near_send.at[0], near_recv.at[0])

    def sum_copy(i):
        peer = lax.rem(row + i, nrows)
        return pltpu.make_async_remote_copy(
            src_ref=sums_ref.at[row],
            dst_ref=sums_ref.at[row],
            send_sem=sum_send.at[i],
            recv_sem=sum_recv.at[row],
            device_id=(me, peer),
            device_id_type=MESH,
        )

    def sum_arrival(i):
        peer = lax.rem(row + i, nrows)
        return pltpu.make_async_remote_copy(
            src_ref=sums_ref.at[peer],
            dst_ref=sums_ref.at[peer],
            send_sem=sum_recv.at[peer],
            recv_sem=sum_recv.at[peer],
            device_id=(me, peer),
            device_id_type=MESH,
        )

    peers = [peer_at(offset) for offset in order]
    for h in range(halves):
        if h:
            fill(h)
        for peer in peers:
            wide_copy(h, peer).start()

    nf = ntm * span
    slab_len = nf // nrows
    contract = (((1,), (1,)), ((), ()))
    cycle_all = owner_ref[...] * 2 + slot_ref[...]
    group = lax.broadcasted_iota(jnp.int32, (nrows, nblocks), 0)
    distances = [lax.rem(row - group + nrows, nrows), lax.rem(group - row + nrows, nrows)]
    pixel_counts = [
        jnp.sum(jnp.where(cycle_all == me * 2 + a, float(width), 0.0), 1, keepdims=True) for a in range(2)
    ]

    def count_of(d, a, first, last):
        inside = (distances[d] >= first) & (distances[d] <= last)
        return jnp.sum(jnp.where(inside, pixel_counts[a], 0.0), 0, keepdims=True)

    def inverse(v):
        return jnp.where(v > 0, 1.0 / jnp.where(v > 0, v, 1.0), 0.0)

    for step in range(STEPS):
        before = [inverse(count_of(d, a, 1, step)) * (1.0 / CODE) for d in range(2) for a in range(2)]
        after = [count_of(d, a, 0, step) * CODE for d in range(2) for a in range(2)]
        count_ref[step] = jnp.concatenate(before + after, 0)
    before = [
        inverse(count_of(d, a, 1, STEPS - (d + a) % 2)) * (1.0 / CODE) for d in range(2) for a in range(2)
    ]
    whole = [count_of(0, a, 0, nrows) for a in range(2)]
    count_ref[STEPS] = jnp.concatenate(before + whole + whole, 0)

    own_entries = [entry_at(me, k) // nblocks for k in range(slots)]
    sums_own = None
    for h in range(halves):
        lines = [
            jnp.concatenate(
                [
                    jnp.full((1, width), jnp.where(e == a + 1, 1.0, 0.0), jnp.float32)
                    for e in own_entries[h * half : (h + 1) * half]
                ],
                1,
            )
            for a in range(2)
        ]
        masks = jnp.concatenate(lines + [jnp.zeros((14, half * width), jnp.float32)], 0)
        masks = masks.astype(jnp.bfloat16)
        wide_batch(h).wait_recv()
        pixels = jnp.concatenate([wide_in[h, :, k].reshape(nf, width) for k in range(half)], 1)
        left = jnp.concatenate([pixels * masks[0:1], pixels * masks[1:2], masks], 0)
        part = lax.dot_general(left, pixels, contract, preferred_element_type=jnp.float32)
        for a in range(2):
            term = part[a * nf : (a + 1) * nf]
            if h:
                gram_ref[a] += term
            else:
                gram_ref[a] = term
        term = part[2 * nf : 2 * nf + 2]
        sums_own = sums_own + term if h else term
    sums_ref[row] = sums_own
    for i in (1, nrows - 1):
        sum_copy(i).start()

    def sums_at(i):
        return sums_ref[lax.rem(row + i, nrows)]

    rows_len = slab_len // PIECES

    def rows_at(slab, piece):
        return pl.ds(pl.multiple_of(slab * slab_len + piece * rows_len, rows_len), rows_len)

    def tall_at(slab, piece, lane):
        return tall_ref[rows_at(slab, piece), lane : lane + 1]

    def own_part(a, slab, piece):
        return gram_ref[a, rows_at(slab, piece), :]

    def ring_copy(flow, step):
        _, way, _, _ = FLOWS[flow]
        return pltpu.make_async_remote_copy(
            src_ref=out_buf.at[flow, step],
            dst_ref=in_buf.at[flow, step],
            send_sem=ring_send.at[flow, step],
            recv_sem=ring_recv.at[flow, step],
            device_id=(me, lax.rem(row + way + nrows, nrows)),
            device_id_type=MESH,
        )

    def tau(b, carry):
        multitau_block(b, near_in, pad_ref, level_ref, corr_ref)
        return carry

    def decode(flow, step, slab, lane, scaled):
        piece = FLOWS[flow][3]
        value = (in_buf[flow, step - 1].astype(jnp.int32) + BIAS).astype(jnp.float32)
        return value * tall_at(slab, piece, lane) * scaled[lane : lane + 1]

    rising = lax.rem(row, STEPS) >= STEPS // 2
    up = jnp.zeros_like(sums_own)
    dn = jnp.zeros_like(sums_own)
    for step in range(STEPS):
        if step:
            sum_arrival(step).wait_recv()
            sum_arrival(nrows - step).wait_recv()
            up = up + sums_at(nrows - step)
            dn = dn + sums_at(step)
        lines = jnp.concatenate([up, dn, inverse(up + sums_own), inverse(dn + sums_own)], 0)
        tall_ref[...] = lines.T
        scaled = lines * count_ref[step][:, 0:1]

        def serve(way_first, step=step, scaled=scaled):
            order = list(range(len(FLOWS)))
            for flow in order:
                a, way, hops, piece = FLOWS[flow]
                if step >= hops:
                    continue
                slab = lax.rem(row + way * (hops - step) + nrows, nrows)
                lane = a if way > 0 else 2 + a
                value = own_part(a, slab, piece)
                if step:
                    ring_copy(flow, step - 1).wait_recv()
                    value = value + decode(flow, step, slab, lane, scaled)
                scale = tall_at(slab, piece, lane + 4)
                code = (value * scale * scaled[lane + 4 : lane + 5] + 0.5).astype(jnp.int32) - BIAS
                out_buf[flow, step] = code.astype(jnp.int16)
                ring_copy(flow, step).start()

        serve(1)
        if step == 0:
            for i in range(2, nrows - 1):
                sum_copy(i).start()
            for peer in peers:
                near_copy(peer).start()

    near_batch.wait_recv()
    lax.fori_loop(0, near, tau, 0)

    for l in range(LEVELS):
        for j in range(lag_ref.shape[1]):
            g2_ref[l * lag_ref.shape[1] + j] = corr_ref[
                l * LAGMAX + jnp.maximum(lag_ref[l, j] - 1, 0)
            ]
    sum_arrival(STEPS).wait_recv()
    last = sums_at(STEPS)
    sums = sums_own + up + dn + last
    ends = [up[0:1] + last[0:1], up[1:2], dn[0:1], dn[1:2] + last[1:2]]
    lines = jnp.concatenate(ends + [sums, sums], 0)
    tall_ref[...] = lines.T
    scaled = lines * count_ref[STEPS][:, 0:1]
    for piece in range(PIECES):
        total = [own_part(a, row, piece) for a in range(2)]
        for flow, (a, way, hops, part) in enumerate(FLOWS):
            if part != piece:
                continue
            ring_copy(flow, hops - 1).wait_recv()
            lane = a if way > 0 else 2 + a
            total[a] = total[a] + decode(flow, hops, row, lane, scaled)
        for a in range(2):
            denom = jnp.maximum(tall_at(row, piece, 4 + a) * sums[a : a + 1], 1.0)
            value = total[a] * (count_ref[STEPS, 4 + a : 5 + a, 0:1] / denom)
            two_ref[pl.ds(piece * rows_len, rows_len), a, :] = value

    for h in range(halves):
        wide_batch(h).wait_send()
    near_batch.wait_send()
    for i in range(1, nrows):
        sum_copy(i).wait_send()
    for flow, (_, _, hops, _) in enumerate(FLOWS):
        for step in range(hops):
            ring_copy(flow, step).wait_send()


def finish(g2_ref, two_ref, g2_out, two_out, sem):
    first = pltpu.make_async_copy(g2_ref, g2_out, sem.at[0])
    second = pltpu.make_async_copy(two_ref, two_out, sem.at[1])
    first.start()
    second.start()
    first.wait()
    second.wait()


def shards(frames, block_owner, cycle_slot, lag_table):
    span, _, nblocks, width = frames.shape
    ntm = lax.axis_size("tm")
    nrows = lax.axis_size("rows")
    cap = 3 * nblocks // ntm
    near = nblocks // ntm
    nf = span * ntm
    slab = nf // nrows
    nflow = len(FLOWS)
    vmem = pl.BlockSpec(memory_space=pltpu.VMEM)
    smem = pl.BlockSpec(memory_space=pltpu.SMEM)
    dma = pltpu.SemaphoreType.DMA
    bf16, f32, i32, i16 = jnp.bfloat16, jnp.float32, jnp.int32, jnp.int16
    g2, two = pl.pallas_call(
        functools.partial(core, ntm, nrows),
        out_shape=(
            pltpu.VMEM((LEVELS * lag_table.shape[1], near, width), f32),
            pltpu.VMEM((slab, 2, nf), f32),
        ),
        in_specs=[smem, vmem, vmem, pl.BlockSpec(memory_space=pl.ANY)],
        out_specs=(vmem, vmem),
        scratch_shapes=[
            pltpu.VMEM((span, nblocks, width), bf16),
            pltpu.VMEM((span * nblocks, width), f32),
            pltpu.VMEM((nblocks, span, width), bf16),
            pltpu.VMEM((2, ntm, cap // 2, span, width), bf16),
            pltpu.VMEM((2, ntm, cap // 2, span, width), bf16),
            pltpu.VMEM((ntm, near, span, width), bf16),
            pltpu.VMEM((8, nblocks), i32),
            pltpu.SMEM((8, nblocks), i32),
            pltpu.VMEM((nf + 64, width), f32),
            pltpu.VMEM((LEVELS - 1, nf // 16 + LAGMAX, 8, width), f32),
            pltpu.VMEM((LEVELS * LAGMAX, near, width), f32),
            pltpu.VMEM((2, nf, nf), f32),
            pltpu.VMEM((nrows, 2, nf), f32),
            pltpu.VMEM((nf, 8), f32),
            pltpu.VMEM((STEPS + 1, 8, nblocks), f32),
            pltpu.VMEM((nflow, STEPS, slab // PIECES, nf), i16),
            pltpu.VMEM((nflow, STEPS, slab // PIECES, nf), i16),
            dma((2,)),
            dma((2,)),
            dma((2,)),
            dma((1,)),
            dma((1,)),
            dma((nrows,)),
            dma((nrows,)),
            dma((nflow, STEPS)),
            dma((nflow, STEPS)),
        ],
        compiler_params=pltpu.CompilerParams(collective_id=0, has_side_effects=True),
    )(lag_table, block_owner[:, :, 0], cycle_slot, frames)
    g2 = pltpu.with_memory_space_constraint(g2, pltpu.VMEM)
    two = pltpu.with_memory_space_constraint(two, pltpu.VMEM)
    hbm = pl.BlockSpec(memory_space=pl.ANY)
    g2, two = pl.pallas_call(
        finish,
        out_shape=(jax.ShapeDtypeStruct(g2.shape, f32), jax.ShapeDtypeStruct(two.shape, f32)),
        in_specs=[vmem, vmem],
        out_specs=(hbm, hbm),
        scratch_shapes=[dma((2,))],
    )(g2, two)
    return g2[None], two


def solution(mesh):
    in_specs = (P("tm", "rows", None, None), P(), P(), P())
    out_specs = (P("rows", None, "tm", None), P("rows", "tm", None))
    return jax.shard_map(shards, mesh=mesh, in_specs=in_specs, out_specs=out_specs, check_vma=False)
```

```python
import functools

import jax
import jax.numpy as jnp
from jax import lax
from jax.experimental import pallas as pl
from jax.experimental.pallas import tpu as pltpu
from jax.sharding import PartitionSpec as P

CYCLES = 64
LEVELS = 4
LAGMAX = 8
MESH = pl.DeviceIdType.MESH
PIECES = 2
CHAINS = ((0, 1, 4), (1, -1, 4), (0, -1, 3), (1, 1, 3))
FLOWS = tuple((a, way, hops, piece) for piece in range(PIECES) for a, way, hops in CHAINS)
STEPS = 4
CODE = 14500.0
BIAS = 32767


def multitau_block(b, recv_ref, pad_ref, level_ref, table_ref):
    nf = recv_ref.shape[0] * recv_ref.shape[2]
    width = recv_ref.shape[3]
    pad_ref[pl.ds(0, nf), :] = recv_ref[:, b].astype(jnp.float32).reshape(nf, width)
    sub = lax.broadcasted_iota(jnp.int32, (8, width), 0)
    for level in range(LEVELS):
        length = nf >> level
        cols = length // 8

        def get(q, level=level, cols=cols):
            if level == 0:
                return pad_ref[pl.ds(q, 8, stride=cols), :]
            return level_ref[level - 1, q]

        window = [get(q) for q in range(LAGMAX)]
        products = [None] * LAGMAX
        total = None
        heads = []
        tails = [None] * LAGMAX
        previous = None
        for q in range(cols):
            window.append(get(q + LAGMAX))
            base = window[q]
            total = base if total is None else total + base
            if q < LAGMAX:
                heads.append(base[0:1])
            if q >= cols - LAGMAX:
                tails[cols - 1 - q] = base[7:8]
            for d in range(1, LAGMAX + 1):
                term = base * window[q + d]
                products[d - 1] = term if products[d - 1] is None else products[d - 1] + term
            if level + 1 < LEVELS:
                if q % 2 == 0:
                    previous = base
                else:
                    mean = (previous + base) * 0.5
                    level_ref[level, q // 2] = mean
                    if q // 2 < LAGMAX:
                        halo = jnp.where(sub < 7, pltpu.roll(mean, 7, 0), 0.0)
                        level_ref[level, cols // 2 + q // 2] = halo
        whole = jnp.sum(total, 0, keepdims=True)
        first, second = whole, whole
        for d in range(1, LAGMAX + 1):
            first = first - tails[d - 1]
            second = second - heads[d - 1]
            product = jnp.sum(products[d - 1], 0, keepdims=True)
            denom = first * second
            safe = jnp.where(denom > 0, denom, 1.0)
            value = jnp.where(denom > 0, product * float(length - d) / safe, 0.0)
            table_ref[level * LAGMAX + d - 1, pl.ds(b, 1), :] = value


def far_first(ny, nx):
    offsets = [(dy, dx, dc) for dy in range(ny) for dx in range(nx) for dc in range(2)][1:]
    order = []
    for dy, dx, dc in sorted(offsets, key=lambda o: -(min(o[0], ny - o[0]) + min(o[1], nx - o[1]))):
        for offset in ((dy, dx, dc), (-dy % ny, -dx % nx, dc)):
            if offset not in order:
                order.append(offset)
    return order


def core(
    ntm,
    nrows,
    lag_ref,
    owner_ref,
    slot_ref,
    frames_ref,
    g2_ref,
    two_ref,
    raw,
    flat,
    near_out,
    wide_out,
    wide_in,
    near_in,
    table_vec,
    table,
    pad_ref,
    level_ref,
    corr_ref,
    gram_ref,
    sums_ref,
    tall_ref,
    count_ref,
    own_buf,
    ratio_buf,
    out_buf,
    in_buf,
    local_sem,
    wide_send,
    wide_recv,
    near_send,
    near_recv,
    sum_send,
    sum_recv,
    ring_send,
    ring_recv,
):
    me = lax.axis_index("tm")
    row = lax.axis_index("rows")
    nx = 4
    ny = ntm // (2 * nx)
    barrier = pltpu.get_barrier_semaphore()
    y, x, c = me // (2 * nx), (me // 2) % nx, me % 2

    def peer_at(offset):
        dy, dx, dc = offset
        return (lax.rem(y + dy, ny) * nx + lax.rem(x + dx, nx)) * 2 + lax.rem(c + dc, 2)

    peers = [peer_at(offset) for offset in far_first(ny, nx)]
    for peer in peers:
        pl.semaphore_signal(barrier, inc=1, device_id=(peer, row), device_id_type=MESH)
    for i in sorted(range(1, nrows), key=lambda i: -min(i, nrows - i)):
        peer = lax.rem(row + i, nrows)
        pl.semaphore_signal(barrier, inc=1, device_id=(me, peer), device_id_type=MESH)
    load = pltpu.make_async_copy(frames_ref.at[:, 0], raw, local_sem.at[0])
    load.start()

    span, nblocks, width = raw.shape
    halves, _, half = wide_in.shape[:3]
    slots = halves * half
    pitch = 16
    near = near_in.shape[1]
    square = (nblocks, nblocks)
    owners = owner_ref[pl.ds(row, 1), :].astype(jnp.float32)
    cycles = slot_ref[pl.ds(row, 1), :].astype(jnp.float32)
    down = lax.broadcasted_iota(jnp.int32, square, 0)
    along = lax.broadcasted_iota(jnp.int32, square, 1)
    alongf = along.astype(jnp.float32)
    across = jnp.broadcast_to(owners, square)
    same = (across == across.T) & (down < along)
    rank = jnp.sum(jnp.where(same, 1.0, 0.0), 0, keepdims=True)
    place = jnp.broadcast_to(owners * float(pitch) + rank, square).T
    entry = jnp.broadcast_to(alongf[0:1] + float(nblocks) * (1.0 + cycles), square).T
    parts = ntm * pitch // nblocks
    rows_of = [
        jnp.sum(jnp.where(place == alongf + float(j * nblocks), entry, 0.0), 0, keepdims=True)
        for j in range(parts)
    ]
    table_vec[...] = jnp.concatenate(
        rows_of + [jnp.zeros((8 - parts, nblocks), jnp.float32)], 0
    ).astype(jnp.int32)
    fetch = pltpu.make_async_copy(table_vec, table, local_sem.at[1])
    fetch.start()
    pad_ref[...] = jnp.zeros_like(pad_ref)
    load.wait()
    flat[...] = raw[...].astype(jnp.float32).reshape(span * nblocks, width)

    def turn(b, carry):
        near_out[b] = flat[pl.ds(b, span, stride=nblocks), :].astype(jnp.bfloat16)
        return carry

    lax.fori_loop(0, nblocks, turn, 0, unroll=8)
    fetch.wait()

    per = nblocks // pitch

    def entry_at(owner, k):
        return table[owner // per, (owner % per) * pitch + k]

    def fill(h):
        def place_owner(o, carry):
            tiles = [near_out[entry_at(o, h * half + k) & (nblocks - 1)] for k in range(half)]
            for k in range(half):
                wide_out[h, o, k] = tiles[k]
            return carry

        lax.fori_loop(0, ntm, place_owner, 0, unroll=2)
        wide_in[h, me] = wide_out[h, me]

    fill(0)
    near_in[me] = near_out[pl.ds(pl.multiple_of(me * near, near), near)]
    pl.semaphore_wait(barrier, ntm + nrows - 2)

    def wide_copy(h, peer):
        return pltpu.make_async_remote_copy(
            src_ref=wide_out.at[h, peer],
            dst_ref=wide_in.at[h, me],
            send_sem=wide_send.at[h],
            recv_sem=wide_recv.at[h],
            device_id=(peer, row),
            device_id_type=MESH,
        )

    def near_copy(peer):
        return pltpu.make_async_remote_copy(
            src_ref=near_out.at[pl.ds(pl.multiple_of(peer * near, near), near)],
            dst_ref=near_in.at[me],
            send_sem=near_send.at[0],
            recv_sem=near_recv.at[0],
            device_id=(peer, row),
            device_id_type=MESH,
        )

    def batch(ref, send, recv):
        return pltpu.make_async_remote_copy(
            src_ref=ref.at[pl.ds(0, ntm - 1)],
            dst_ref=ref.at[pl.ds(0, ntm - 1)],
            send_sem=send,
            recv_sem=recv,
            device_id=(lax.rem(me + 1, ntm), row),
            device_id_type=MESH,
        )

    def wide_batch(h):
        return batch(wide_in.at[h], wide_send.at[h], wide_recv.at[h])

    near_batch = batch(near_in, near_send.at[0], near_recv.at[0])

    def sum_copy(i):
        peer = lax.rem(row + i, nrows)
        return pltpu.make_async_remote_copy(
            src_ref=sums_ref.at[row],
            dst_ref=sums_ref.at[row],
            send_sem=sum_send.at[i],
            recv_sem=sum_recv.at[row],
            device_id=(me, peer),
            device_id_type=MESH,
        )

    def sum_arrival(i):
        peer = lax.rem(row + i, nrows)
        return pltpu.make_async_remote_copy(
            src_ref=sums_ref.at[peer],
            dst_ref=sums_ref.at[peer],
            send_sem=sum_recv.at[peer],
            recv_sem=sum_recv.at[peer],
            device_id=(me, peer),
            device_id_type=MESH,
        )

    for h in range(halves):
        if h:
            fill(h)
        for peer in peers:
            wide_copy(h, peer).start()

    nf = ntm * span
    slab_len = nf // nrows
    contract = (((1,), (1,)), ((), ()))
    cycle_all = owner_ref[...] * 2 + slot_ref[...]
    group = lax.broadcasted_iota(jnp.int32, (nrows, nblocks), 0)
    distances = [lax.rem(row - group + nrows, nrows), lax.rem(group - row + nrows, nrows)]
    pixel_counts = [
        jnp.sum(jnp.where(cycle_all == me * 2 + a, float(width), 0.0), 1, keepdims=True) for a in range(2)
    ]

    def count_of(d, a, first, last):
        inside = (distances[d] >= first) & (distances[d] <= last)
        return jnp.sum(jnp.where(inside, pixel_counts[a], 0.0), 0, keepdims=True)

    def inverse(v):
        return jnp.where(v > 0, 1.0 / jnp.where(v > 0, v, 1.0), 0.0)

    for step in range(STEPS):
        before = [inverse(count_of(d, a, 1, step)) * (1.0 / CODE) for d in range(2) for a in range(2)]
        after = [count_of(d, a, 0, step) * CODE for d in range(2) for a in range(2)]
        count_ref[step] = jnp.concatenate(before + after, 0)
    before = [
        inverse(count_of(d, a, 1, STEPS - (d + a) % 2)) * (1.0 / CODE) for d in range(2) for a in range(2)
    ]
    whole = [count_of(0, a, 0, nrows) for a in range(2)]
    count_ref[STEPS] = jnp.concatenate(before + whole + whole, 0)

    own_entries = [entry_at(me, k) // nblocks for k in range(slots)]
    sums_own = None
    for h in range(halves):
        lines = [
            jnp.concatenate(
                [
                    jnp.full((1, width), jnp.where(e == a + 1, 1.0, 0.0), jnp.float32)
                    for e in own_entries[h * half : (h + 1) * half]
                ],
                1,
            )
            for a in range(2)
        ]
        masks = jnp.concatenate(lines + [jnp.zeros((14, half * width), jnp.float32)], 0)
        masks = masks.astype(jnp.bfloat16)
        wide_batch(h).wait_recv()
        pixels = jnp.concatenate([wide_in[h, :, k].reshape(nf, width) for k in range(half)], 1)
        left = jnp.concatenate([pixels * masks[0:1], pixels * masks[1:2], masks], 0)
        part = lax.dot_general(left, pixels, contract, preferred_element_type=jnp.float32)
        for a in range(2):
            term = part[a * nf : (a + 1) * nf]
            if h:
                gram_ref[a] += term
            else:
                gram_ref[a] = term
        term = part[2 * nf : 2 * nf + 2]
        sums_own = sums_own + term if h else term
    sums_ref[row] = sums_own
    for i in (1, nrows - 1):
        sum_copy(i).start()

    def sums_at(i):
        return sums_ref[lax.rem(row + i, nrows)]

    rows_len = slab_len // PIECES

    def rows_at(slab, piece):
        return pl.ds(pl.multiple_of(slab * slab_len + piece * rows_len, rows_len), rows_len)

    def tall_at(slab, piece, lane):
        return tall_ref[rows_at(slab, piece), lane : lane + 1]

    def own_part(a, slab, piece):
        return gram_ref[a, rows_at(slab, piece), :]

    def ring_copy(flow, step):
        _, way, _, _ = FLOWS[flow]
        return pltpu.make_async_remote_copy(
            src_ref=out_buf.at[flow, step],
            dst_ref=in_buf.at[flow, step],
            send_sem=ring_send.at[flow, step],
            recv_sem=ring_recv.at[flow, step],
            device_id=(me, lax.rem(row + way + nrows, nrows)),
            device_id_type=MESH,
        )

    def tau(b, carry):
        multitau_block(b, near_in, pad_ref, level_ref, corr_ref)
        return carry

    up = jnp.zeros_like(sums_own)
    dn = jnp.zeros_like(sums_own)
    for step in range(STEPS):
        if step:
            sum_arrival(step).wait_recv()
            sum_arrival(nrows - step).wait_recv()
            up = up + sums_at(nrows - step)
            dn = dn + sums_at(step)
        lines = jnp.concatenate([up, dn, inverse(up + sums_own), inverse(dn + sums_own)], 0)
        tall_ref[...] = lines.T
        scaled = lines * count_ref[step][:, 0:1]

        live = [flow for flow in range(len(FLOWS)) if step < FLOWS[flow][2]]
        for flow in live:
            a, way, hops, piece = FLOWS[flow]
            slab = lax.rem(row + way * (hops - step) + nrows, nrows)
            lane = a if way > 0 else 2 + a
            tall = tall_at(slab, piece, lane + 4)
            line = scaled[lane + 4 : lane + 5]
            own = own_part(a, slab, piece) * tall * line + 0.5
            if step:
                ratio = (tall_at(slab, piece, lane) * tall) * (scaled[lane : lane + 1] * line)
                ratio_buf[flow] = ratio
                own_buf[flow] = own + ratio * float(BIAS)
            else:
                out_buf[flow, step] = (own.astype(jnp.int32) - BIAS).astype(jnp.int16)
                ring_copy(flow, step).start()
        if step:
            for flow in live:
                ring_copy(flow, step - 1).wait_recv()
                value = in_buf[flow, step - 1].astype(jnp.int32).astype(jnp.float32)
                code = (value * ratio_buf[flow] + own_buf[flow]).astype(jnp.int32) - BIAS
                out_buf[flow, step] = code.astype(jnp.int16)
                ring_copy(flow, step).start()

        if step == 0:
            for i in range(2, nrows - 1):
                sum_copy(i).start()
            for peer in peers:
                near_copy(peer).start()

    near_batch.wait_recv()
    lax.fori_loop(0, near, tau, 0)

    for l in range(LEVELS):
        for j in range(lag_ref.shape[1]):
            g2_ref[l * lag_ref.shape[1] + j] = corr_ref[
                l * LAGMAX + jnp.maximum(lag_ref[l, j] - 1, 0)
            ]
    sum_arrival(STEPS).wait_recv()
    last = sums_at(STEPS)
    sums = sums_own + up + dn + last
    ends = [up[0:1] + last[0:1], up[1:2], dn[0:1], dn[1:2] + last[1:2]]
    lines = jnp.concatenate(ends + [sums, sums], 0)
    tall_ref[...] = lines.T
    scaled = lines * count_ref[STEPS][:, 0:1]
    for piece in range(PIECES):
        for a in range(2):
            denom = jnp.maximum(tall_at(row, piece, 4 + a) * sums[a : a + 1], 1.0)
            weight = count_ref[STEPS, 4 + a : 5 + a, 0:1] / denom
            own = own_part(a, row, piece) * weight
            for d in range(2):
                flow = FLOWS.index((a, 1 - 2 * d, STEPS - (a + d) % 2, piece))
                lane = 2 * d + a
                ratio = tall_at(row, piece, lane) * scaled[lane : lane + 1] * weight
                ratio_buf[flow] = ratio
                own = own + ratio * float(BIAS)
            own_buf[FLOWS.index((a, 1, STEPS - a, piece))] = own
    for piece in range(PIECES):
        for a in range(2):
            value = own_buf[FLOWS.index((a, 1, STEPS - a, piece))]
            for hops in (STEPS - 1, STEPS):
                way = 1 if hops == STEPS - a else -1
                flow = FLOWS.index((a, way, hops, piece))
                ring_copy(flow, hops - 1).wait_recv()
                code = in_buf[flow, hops - 1].astype(jnp.int32).astype(jnp.float32)
                value = value + code * ratio_buf[flow]
            two_ref[pl.ds(piece * rows_len, rows_len), a, :] = value

    for h in range(halves):
        wide_batch(h).wait_send()
    near_batch.wait_send()
    for i in range(1, nrows):
        sum_copy(i).wait_send()
    for flow, (_, _, hops, _) in enumerate(FLOWS):
        for step in range(hops):
            ring_copy(flow, step).wait_send()


def finish(g2_ref, two_ref, g2_out, two_out, sem):
    first = pltpu.make_async_copy(g2_ref, g2_out, sem.at[0])
    second = pltpu.make_async_copy(two_ref, two_out, sem.at[1])
    first.start()
    second.start()
    first.wait()
    second.wait()


def shards(frames, block_owner, cycle_slot, lag_table):
    span, _, nblocks, width = frames.shape
    ntm = lax.axis_size("tm")
    nrows = lax.axis_size("rows")
    cap = 3 * nblocks // ntm
    near = nblocks // ntm
    nf = span * ntm
    slab = nf // nrows
    nflow = len(FLOWS)
    vmem = pl.BlockSpec(memory_space=pltpu.VMEM)
    smem = pl.BlockSpec(memory_space=pltpu.SMEM)
    dma = pltpu.SemaphoreType.DMA
    bf16, f32, i32, i16 = jnp.bfloat16, jnp.float32, jnp.int32, jnp.int16
    g2, two = pl.pallas_call(
        functools.partial(core, ntm, nrows),
        out_shape=(
            pltpu.VMEM((LEVELS * lag_table.shape[1], near, width), f32),
            pltpu.VMEM((slab, 2, nf), f32),
        ),
        in_specs=[smem, vmem, vmem, pl.BlockSpec(memory_space=pl.ANY)],
        out_specs=(vmem, vmem),
        scratch_shapes=[
            pltpu.VMEM((span, nblocks, width), bf16),
            pltpu.VMEM((span * nblocks, width), f32),
            pltpu.VMEM((nblocks, span, width), bf16),
            pltpu.VMEM((2, ntm, cap // 2, span, width), bf16),
            pltpu.VMEM((2, ntm, cap // 2, span, width), bf16),
            pltpu.VMEM((ntm, near, span, width), bf16),
            pltpu.VMEM((8, nblocks), i32),
            pltpu.SMEM((8, nblocks), i32),
            pltpu.VMEM((nf + 64, width), f32),
            pltpu.VMEM((LEVELS - 1, nf // 16 + LAGMAX, 8, width), f32),
            pltpu.VMEM((LEVELS * LAGMAX, near, width), f32),
            pltpu.VMEM((2, nf, nf), f32),
            pltpu.VMEM((nrows, 2, nf), f32),
            pltpu.VMEM((nf, 8), f32),
            pltpu.VMEM((STEPS + 1, 8, nblocks), f32),
            pltpu.VMEM((nflow, slab // PIECES, nf), f32),
            pltpu.VMEM((nflow, slab // PIECES, nf), f32),
            pltpu.VMEM((nflow, STEPS, slab // PIECES, nf), i16),
            pltpu.VMEM((nflow, STEPS, slab // PIECES, nf), i16),
            dma((2,)),
            dma((2,)),
            dma((2,)),
            dma((1,)),
            dma((1,)),
            dma((nrows,)),
            dma((nrows,)),
            dma((nflow, STEPS)),
            dma((nflow, STEPS)),
        ],
        compiler_params=pltpu.CompilerParams(collective_id=0, has_side_effects=True),
    )(lag_table, block_owner[:, :, 0], cycle_slot, frames)
    g2 = pltpu.with_memory_space_constraint(g2, pltpu.VMEM)
    two = pltpu.with_memory_space_constraint(two, pltpu.VMEM)
    hbm = pl.BlockSpec(memory_space=pl.ANY)
    g2, two = pl.pallas_call(
        finish,
        out_shape=(jax.ShapeDtypeStruct(g2.shape, f32), jax.ShapeDtypeStruct(two.shape, f32)),
        in_specs=[vmem, vmem],
        out_specs=(hbm, hbm),
        scratch_shapes=[dma((2,))],
    )(g2, two)
    return g2[None], two


def solution(mesh):
    in_specs = (P("tm", "rows", None, None), P(), P(), P())
    out_specs = (P("rows", None, "tm", None), P("rows", "tm", None))
    return jax.shard_map(shards, mesh=mesh, in_specs=in_specs, out_specs=out_specs, check_vma=False)
```

```python
import functools

import jax
import jax.numpy as jnp
from jax import lax
from jax.experimental import pallas as pl
from jax.experimental.pallas import tpu as pltpu
from jax.sharding import PartitionSpec as P

CYCLES = 64
LEVELS = 4
LAGMAX = 8
MESH = pl.DeviceIdType.MESH
PIECES = 2
CHAINS = ((0, 1, 4), (1, -1, 4), (0, -1, 3), (1, 1, 3))
FLOWS = tuple((a, way, hops, piece) for piece in range(PIECES) for a, way, hops in CHAINS)
STEPS = 4
FIRST = tuple(sum(flow[2] for flow in FLOWS[:i]) for i in range(len(FLOWS) + 1))
MESSAGES = FIRST[-1]
CODE = 14500.0
BIAS = 32767


def multitau_block(b, recv_ref, pad_ref, level_ref, table_ref):
    nf = recv_ref.shape[0] * recv_ref.shape[2]
    width = recv_ref.shape[3]
    pad_ref[pl.ds(0, nf), :] = recv_ref[:, b].astype(jnp.float32).reshape(nf, width)
    sub = lax.broadcasted_iota(jnp.int32, (8, width), 0)
    for level in range(LEVELS):
        length = nf >> level
        cols = length // 8

        def get(q, level=level, cols=cols):
            if level == 0:
                return pad_ref[pl.ds(q, 8, stride=cols), :]
            return level_ref[level - 1, q]

        window = [get(q) for q in range(LAGMAX)]
        products = [None] * LAGMAX
        total = None
        heads = []
        tails = [None] * LAGMAX
        previous = None
        for q in range(cols):
            window.append(get(q + LAGMAX))
            base = window[q]
            total = base if total is None else total + base
            if q < LAGMAX:
                heads.append(base[0:1])
            if q >= cols - LAGMAX:
                tails[cols - 1 - q] = base[7:8]
            for d in range(1, LAGMAX + 1):
                term = base * window[q + d]
                products[d - 1] = term if products[d - 1] is None else products[d - 1] + term
            if level + 1 < LEVELS:
                if q % 2 == 0:
                    previous = base
                else:
                    mean = (previous + base) * 0.5
                    level_ref[level, q // 2] = mean
                    if q // 2 < LAGMAX:
                        halo = jnp.where(sub < 7, pltpu.roll(mean, 7, 0), 0.0)
                        level_ref[level, cols // 2 + q // 2] = halo
        whole = jnp.sum(total, 0, keepdims=True)
        first, second = whole, whole
        for d in range(1, LAGMAX + 1):
            first = first - tails[d - 1]
            second = second - heads[d - 1]
            product = jnp.sum(products[d - 1], 0, keepdims=True)
            denom = first * second
            safe = jnp.where(denom > 0, denom, 1.0)
            value = jnp.where(denom > 0, product * float(length - d) / safe, 0.0)
            table_ref[level * LAGMAX + d - 1, pl.ds(b, 1), :] = value


def far_first(ny, nx):
    offsets = [(dy, dx, dc) for dy in range(ny) for dx in range(nx) for dc in range(2)][1:]
    order = []
    for dy, dx, dc in sorted(offsets, key=lambda o: -(min(o[0], ny - o[0]) + min(o[1], nx - o[1]))):
        for offset in ((dy, dx, dc), (-dy % ny, -dx % nx, dc)):
            if offset not in order:
                order.append(offset)
    return order


def core(
    ntm,
    nrows,
    lag_ref,
    owner_ref,
    slot_ref,
    frames_ref,
    g2_ref,
    two_ref,
    raw,
    flat,
    near_out,
    wide_out,
    wide_in,
    near_in,
    table_vec,
    table,
    pad_ref,
    level_ref,
    corr_ref,
    gram_ref,
    sums_ref,
    tall_ref,
    count_ref,
    own_buf,
    ratio_buf,
    out_buf,
    in_buf,
    local_sem,
    wide_send,
    wide_recv,
    near_send,
    near_recv,
    sum_send,
    sum_recv,
    ring_send,
    ring_recv,
):
    me = lax.axis_index("tm")
    row = lax.axis_index("rows")
    nx = 4
    ny = ntm // (2 * nx)
    barrier = pltpu.get_barrier_semaphore()
    load = pltpu.make_async_copy(frames_ref.at[:, 0], raw, local_sem.at[0])
    load.start()
    y, x, c = me // (2 * nx), (me // 2) % nx, me % 2

    def peer_at(offset):
        dy, dx, dc = offset
        return (lax.rem(y + dy, ny) * nx + lax.rem(x + dx, nx)) * 2 + lax.rem(c + dc, 2)

    def wrapped(value, size):
        return jnp.where(value >= size, value - size, value)

    for i in sorted(range(1, ntm), key=lambda i: -(min(i // 8, 4 - i // 8) + min(i // 2 % 4, 4 - i // 2 % 4))):
        peer = wrapped(me + i, ntm)
        pl.semaphore_signal(barrier, inc=1, device_id=(peer, row), device_id_type=MESH)
    for i in sorted(range(1, nrows), key=lambda i: -min(i, nrows - i)):
        peer = wrapped(row + i, nrows)
        pl.semaphore_signal(barrier, inc=1, device_id=(me, peer), device_id_type=MESH)

    span, nblocks, width = raw.shape
    halves, _, half = wide_in.shape[:3]
    slots = halves * half
    pitch = 16
    near = near_in.shape[1]
    square = (nblocks, nblocks)
    owners = owner_ref[pl.ds(row, 1), :].astype(jnp.float32)
    cycles = slot_ref[pl.ds(row, 1), :].astype(jnp.float32)
    down = lax.broadcasted_iota(jnp.int32, square, 0)
    along = lax.broadcasted_iota(jnp.int32, square, 1)
    alongf = along.astype(jnp.float32)
    across = jnp.broadcast_to(owners, square)
    same = (across == across.T) & (down < along)
    rank = jnp.sum(jnp.where(same, 1.0, 0.0), 0, keepdims=True)
    place = jnp.broadcast_to(owners * float(pitch) + rank, square).T
    entry = jnp.broadcast_to(alongf[0:1] + float(nblocks) * (1.0 + cycles), square).T
    parts = ntm * pitch // nblocks
    rows_of = [
        jnp.sum(jnp.where(place == alongf + float(j * nblocks), entry, 0.0), 0, keepdims=True)
        for j in range(parts)
    ]
    table_vec[...] = jnp.concatenate(
        rows_of + [jnp.zeros((8 - parts, nblocks), jnp.float32)], 0
    ).astype(jnp.int32)
    fetch = pltpu.make_async_copy(table_vec, table, local_sem.at[1])
    fetch.start()
    pad_ref[...] = jnp.zeros_like(pad_ref)
    load.wait()
    flat[...] = raw[...].astype(jnp.float32).reshape(span * nblocks, width)

    def turn(b, carry):
        near_out[b] = flat[pl.ds(b, span, stride=nblocks), :].astype(jnp.bfloat16)
        return carry

    lax.fori_loop(0, nblocks, turn, 0, unroll=8)
    fetch.wait()

    per = nblocks // pitch

    def entry_at(owner, k):
        return table[owner // per, (owner % per) * pitch + k]

    def fill(h):
        def place_owner(o, carry):
            tiles = [near_out[entry_at(o, h * half + k) & (nblocks - 1)] for k in range(half)]
            for k in range(half):
                wide_out[h, o, k] = tiles[k]
            return carry

        lax.fori_loop(0, ntm, place_owner, 0, unroll=2)
        wide_in[h, me] = wide_out[h, me]

    fill(0)
    near_in[me] = near_out[pl.ds(pl.multiple_of(me * near, near), near)]
    pl.semaphore_wait(barrier, ntm + nrows - 2)

    peers = [peer_at(offset) for offset in far_first(ny, nx)]

    def wide_copy(h, peer):
        return pltpu.make_async_remote_copy(
            src_ref=wide_out.at[h, peer],
            dst_ref=wide_in.at[h, me],
            send_sem=wide_send.at[h],
            recv_sem=wide_recv.at[h],
            device_id=(peer, row),
            device_id_type=MESH,
        )

    def near_copy(peer):
        return pltpu.make_async_remote_copy(
            src_ref=near_out.at[pl.ds(pl.multiple_of(peer * near, near), near)],
            dst_ref=near_in.at[me],
            send_sem=near_send.at[0],
            recv_sem=near_recv.at[0],
            device_id=(peer, row),
            device_id_type=MESH,
        )

    def batch(ref, send, recv):
        return pltpu.make_async_remote_copy(
            src_ref=ref.at[pl.ds(0, ntm - 1)],
            dst_ref=ref.at[pl.ds(0, ntm - 1)],
            send_sem=send,
            recv_sem=recv,
            device_id=(lax.rem(me + 1, ntm), row),
            device_id_type=MESH,
        )

    def wide_batch(h):
        return batch(wide_in.at[h], wide_send.at[h], wide_recv.at[h])

    near_batch = batch(near_in, near_send.at[0], near_recv.at[0])

    def sum_copy(i):
        peer = lax.rem(row + i, nrows)
        return pltpu.make_async_remote_copy(
            src_ref=sums_ref.at[row],
            dst_ref=sums_ref.at[row],
            send_sem=sum_send.at[0],
            recv_sem=sum_recv.at[row],
            device_id=(me, peer),
            device_id_type=MESH,
        )

    def sum_arrival(i):
        peer = lax.rem(row + i, nrows)
        return pltpu.make_async_remote_copy(
            src_ref=sums_ref.at[peer],
            dst_ref=sums_ref.at[peer],
            send_sem=sum_recv.at[peer],
            recv_sem=sum_recv.at[peer],
            device_id=(me, peer),
            device_id_type=MESH,
        )

    for h in range(halves):
        if h:
            fill(h)
        for peer in peers:
            wide_copy(h, peer).start()

    nf = ntm * span
    slab_len = nf // nrows
    contract = (((1,), (1,)), ((), ()))
    cycle_all = owner_ref[...] * 2 + slot_ref[...]
    group = lax.broadcasted_iota(jnp.int32, (nrows, nblocks), 0)
    distances = [lax.rem(row - group + nrows, nrows), lax.rem(group - row + nrows, nrows)]
    pixel_counts = [
        jnp.sum(jnp.where(cycle_all == me * 2 + a, float(width), 0.0), 1, keepdims=True) for a in range(2)
    ]

    def count_of(d, a, first, last):
        inside = (distances[d] >= first) & (distances[d] <= last)
        return jnp.sum(jnp.where(inside, pixel_counts[a], 0.0), 0, keepdims=True)

    def inverse(v):
        return jnp.where(v > 0, 1.0 / jnp.where(v > 0, v, 1.0), 0.0)

    for step in range(STEPS):
        before = [inverse(count_of(d, a, 1, step)) * (1.0 / CODE) for d in range(2) for a in range(2)]
        after = [count_of(d, a, 0, step) * CODE for d in range(2) for a in range(2)]
        count_ref[step] = jnp.concatenate(before + after, 0)
    before = [
        inverse(count_of(d, a, 1, STEPS - (d + a) % 2)) * (1.0 / CODE) for d in range(2) for a in range(2)
    ]
    whole = [count_of(0, a, 0, nrows) for a in range(2)]
    count_ref[STEPS] = jnp.concatenate(before + whole + whole, 0)

    own_entries = [entry_at(me, k) // nblocks for k in range(slots)]
    sums_own = None
    for h in range(halves):
        lines = [
            jnp.concatenate(
                [
                    jnp.full((1, width), jnp.where(e == a + 1, 1.0, 0.0), jnp.float32)
                    for e in own_entries[h * half : (h + 1) * half]
                ],
                1,
            )
            for a in range(2)
        ]
        masks = jnp.concatenate(lines + [jnp.zeros((14, half * width), jnp.float32)], 0)
        masks = masks.astype(jnp.bfloat16)
        wide_batch(h).wait_recv()
        pixels = jnp.concatenate([wide_in[h, :, k].reshape(nf, width) for k in range(half)], 1)
        left = jnp.concatenate([pixels * masks[0:1], pixels * masks[1:2], masks], 0)
        part = lax.dot_general(left, pixels, contract, preferred_element_type=jnp.float32)
        for a in range(2):
            term = part[a * nf : (a + 1) * nf]
            if h:
                gram_ref[a] += term
            else:
                gram_ref[a] = term
        term = part[2 * nf : 2 * nf + 2]
        sums_own = sums_own + term if h else term
    sums_ref[row] = sums_own
    for i in (1, nrows - 1):
        sum_copy(i).start()

    def sums_at(i):
        return sums_ref[lax.rem(row + i, nrows)]

    rows_len = slab_len // PIECES

    def rows_at(slab, piece):
        return pl.ds(pl.multiple_of(slab * slab_len + piece * rows_len, rows_len), rows_len)

    def tall_at(slab, piece, lane):
        return tall_ref[rows_at(slab, piece), lane : lane + 1]

    def own_part(a, slab, piece):
        return gram_ref[a, rows_at(slab, piece), :]

    def ring_copy(flow, step):
        _, way, _, _ = FLOWS[flow]
        return pltpu.make_async_remote_copy(
            src_ref=out_buf.at[FIRST[flow] + step],
            dst_ref=in_buf.at[FIRST[flow] + step],
            send_sem=ring_send.at[0],
            recv_sem=ring_recv.at[FIRST[flow] + step],
            device_id=(me, lax.rem(row + way + nrows, nrows)),
            device_id_type=MESH,
        )

    def tau(b, carry):
        multitau_block(b, near_in, pad_ref, level_ref, corr_ref)
        return carry

    up = jnp.zeros_like(sums_own)
    dn = jnp.zeros_like(sums_own)
    for step in range(STEPS):
        if step:
            sum_arrival(step).wait_recv()
            sum_arrival(nrows - step).wait_recv()
            up = up + sums_at(nrows - step)
            dn = dn + sums_at(step)
        lines = jnp.concatenate([up, dn, inverse(up + sums_own), inverse(dn + sums_own)], 0)
        tall_ref[...] = lines.T
        scaled = lines * count_ref[step][:, 0:1]

        live = [flow for flow in range(len(FLOWS)) if step < FLOWS[flow][2]]
        for flow in live:
            a, way, hops, piece = FLOWS[flow]
            slab = lax.rem(row + way * (hops - step) + nrows, nrows)
            lane = a if way > 0 else 2 + a
            tall = tall_at(slab, piece, lane + 4)
            line = scaled[lane + 4 : lane + 5]
            own = own_part(a, slab, piece) * tall * line + 0.5
            if step:
                ratio = (tall_at(slab, piece, lane) * tall) * (scaled[lane : lane + 1] * line)
                ratio_buf[flow] = ratio
                own_buf[flow] = own + ratio * float(BIAS)
            else:
                out_buf[FIRST[flow] + step] = (own.astype(jnp.int32) - BIAS).astype(jnp.int16)
                ring_copy(flow, step).start()
        if step:
            for flow in live:
                ring_copy(flow, step - 1).wait_recv()
                value = in_buf[FIRST[flow] + step - 1].astype(jnp.int32).astype(jnp.float32)
                code = (value * ratio_buf[flow] + own_buf[flow]).astype(jnp.int32) - BIAS
                out_buf[FIRST[flow] + step] = code.astype(jnp.int16)
                ring_copy(flow, step).start()

        if step == 0:
            for i in range(2, nrows - 1):
                sum_copy(i).start()
            for peer in peers:
                near_copy(peer).start()

    near_batch.wait_recv()
    lax.fori_loop(0, near, tau, 0)

    for l in range(LEVELS):
        for j in range(lag_ref.shape[1]):
            g2_ref[l * lag_ref.shape[1] + j] = corr_ref[
                l * LAGMAX + jnp.maximum(lag_ref[l, j] - 1, 0)
            ]
    sum_arrival(STEPS).wait_recv()
    last = sums_at(STEPS)
    sums = sums_own + up + dn + last
    ends = [up[0:1] + last[0:1], up[1:2], dn[0:1], dn[1:2] + last[1:2]]
    lines = jnp.concatenate(ends + [sums, sums], 0)
    tall_ref[...] = lines.T
    scaled = lines * count_ref[STEPS][:, 0:1]
    for piece in range(PIECES):
        for a in range(2):
            denom = jnp.maximum(tall_at(row, piece, 4 + a) * sums[a : a + 1], 1.0)
            weight = count_ref[STEPS, 4 + a : 5 + a, 0:1] / denom
            own = own_part(a, row, piece) * weight
            for d in range(2):
                flow = FLOWS.index((a, 1 - 2 * d, STEPS - (a + d) % 2, piece))
                lane = 2 * d + a
                ratio = tall_at(row, piece, lane) * scaled[lane : lane + 1] * weight
                ratio_buf[flow] = ratio
                own = own + ratio * float(BIAS)
            own_buf[FLOWS.index((a, 1, STEPS - a, piece))] = own
    for piece in range(PIECES):
        for a in range(2):
            value = own_buf[FLOWS.index((a, 1, STEPS - a, piece))]
            for hops in (STEPS - 1, STEPS):
                way = 1 if hops == STEPS - a else -1
                flow = FLOWS.index((a, way, hops, piece))
                ring_copy(flow, hops - 1).wait_recv()
                code = in_buf[FIRST[flow] + hops - 1].astype(jnp.int32).astype(jnp.float32)
                value = value + code * ratio_buf[flow]
            two_ref[pl.ds(piece * rows_len, rows_len), a, :] = value

    for h in range(halves):
        wide_batch(h).wait_send()
    near_batch.wait_send()
    for ref, sem, total in (
        (sums_ref, sum_send.at[0], nrows - 1),
        (out_buf, ring_send.at[0], MESSAGES),
    ):
        sent = ref.at[pl.ds(0, total)]
        pltpu.make_async_remote_copy(
            src_ref=sent,
            dst_ref=sent,
            send_sem=sem,
            recv_sem=sem,
            device_id=(me, lax.rem(row + 1, nrows)),
            device_id_type=MESH,
        ).wait_send()


def finish(g2_ref, two_ref, g2_out, two_out, sem):
    first = pltpu.make_async_copy(g2_ref, g2_out, sem.at[0])
    second = pltpu.make_async_copy(two_ref, two_out, sem.at[1])
    first.start()
    second.start()
    first.wait()
    second.wait()


def shards(frames, block_owner, cycle_slot, lag_table):
    span, _, nblocks, width = frames.shape
    ntm = lax.axis_size("tm")
    nrows = lax.axis_size("rows")
    cap = 3 * nblocks // ntm
    near = nblocks // ntm
    nf = span * ntm
    slab = nf // nrows
    nflow = len(FLOWS)
    vmem = pl.BlockSpec(memory_space=pltpu.VMEM)
    smem = pl.BlockSpec(memory_space=pltpu.SMEM)
    dma = pltpu.SemaphoreType.DMA
    bf16, f32, i32, i16 = jnp.bfloat16, jnp.float32, jnp.int32, jnp.int16
    g2, two = pl.pallas_call(
        functools.partial(core, ntm, nrows),
        out_shape=(
            pltpu.VMEM((LEVELS * lag_table.shape[1], near, width), f32),
            pltpu.VMEM((slab, 2, nf), f32),
        ),
        in_specs=[smem, vmem, vmem, pl.BlockSpec(memory_space=pl.ANY)],
        out_specs=(vmem, vmem),
        scratch_shapes=[
            pltpu.VMEM((span, nblocks, width), bf16),
            pltpu.VMEM((span * nblocks, width), f32),
            pltpu.VMEM((nblocks, span, width), bf16),
            pltpu.VMEM((2, ntm, cap // 2, span, width), bf16),
            pltpu.VMEM((2, ntm, cap // 2, span, width), bf16),
            pltpu.VMEM((ntm, near, span, width), bf16),
            pltpu.VMEM((8, nblocks), i32),
            pltpu.SMEM((8, nblocks), i32),
            pltpu.VMEM((nf + 64, width), f32),
            pltpu.VMEM((LEVELS - 1, nf // 16 + LAGMAX, 8, width), f32),
            pltpu.VMEM((LEVELS * LAGMAX, near, width), f32),
            pltpu.VMEM((2, nf, nf), f32),
            pltpu.VMEM((nrows, 2, nf), f32),
            pltpu.VMEM((nf, 8), f32),
            pltpu.VMEM((STEPS + 1, 8, nblocks), f32),
            pltpu.VMEM((nflow, slab // PIECES, nf), f32),
            pltpu.VMEM((nflow, slab // PIECES, nf), f32),
            pltpu.VMEM((MESSAGES, slab // PIECES, nf), i16),
            pltpu.VMEM((MESSAGES, slab // PIECES, nf), i16),
            dma((2,)),
            dma((2,)),
            dma((2,)),
            dma((1,)),
            dma((1,)),
            dma((1,)),
            dma((nrows,)),
            dma((1,)),
            dma((MESSAGES,)),
        ],
        compiler_params=pltpu.CompilerParams(collective_id=0, has_side_effects=True),
    )(lag_table, block_owner[:, :, 0], cycle_slot, frames)
    g2 = pltpu.with_memory_space_constraint(g2, pltpu.VMEM)
    two = pltpu.with_memory_space_constraint(two, pltpu.VMEM)
    hbm = pl.BlockSpec(memory_space=pl.ANY)
    g2, two = pl.pallas_call(
        finish,
        out_shape=(jax.ShapeDtypeStruct(g2.shape, f32), jax.ShapeDtypeStruct(two.shape, f32)),
        in_specs=[vmem, vmem],
        out_specs=(hbm, hbm),
        scratch_shapes=[dma((2,))],
    )(g2, two)
    return g2[None], two


def solution(mesh):
    in_specs = (P("tm", "rows", None, None), P(), P(), P())
    out_specs = (P("rows", None, "tm", None), P("rows", "tm", None))
    return jax.shard_map(shards, mesh=mesh, in_specs=in_specs, out_specs=out_specs, check_vma=False)
```

```python
import functools

import jax
import jax.numpy as jnp
from jax import lax
from jax.experimental import pallas as pl
from jax.experimental.pallas import tpu as pltpu
from jax.sharding import PartitionSpec as P

CYCLES = 64
LEVELS = 4
LAGMAX = 8
MESH = pl.DeviceIdType.MESH
PIECES = 2
CHAINS = ((0, 1, 4), (1, -1, 4), (0, -1, 3), (1, 1, 3))
FLOWS = tuple((a, way, hops, piece) for a, way, hops in CHAINS for piece in range(PIECES))
STEPS = 4
FIRST = tuple(sum(flow[2] for flow in FLOWS[:i]) for i in range(len(FLOWS) + 1))
MESSAGES = FIRST[-1]
CODE = 14500.0
BIAS = 32767


def multitau_block(b, recv_ref, pad_ref, level_ref, table_ref):
    nf = recv_ref.shape[0] * recv_ref.shape[2]
    width = recv_ref.shape[3]
    pad_ref[pl.ds(0, nf), :] = recv_ref[:, b].astype(jnp.float32).reshape(nf, width)
    sub = lax.broadcasted_iota(jnp.int32, (8, width), 0)
    for level in range(LEVELS):
        length = nf >> level
        cols = length // 8

        def get(q, level=level, cols=cols):
            if level == 0:
                return pad_ref[pl.ds(q, 8, stride=cols), :]
            return level_ref[level - 1, q]

        window = [get(q) for q in range(LAGMAX)]
        products = [None] * LAGMAX
        total = None
        heads = []
        tails = [None] * LAGMAX
        previous = None
        for q in range(cols):
            window.append(get(q + LAGMAX))
            base = window[q]
            total = base if total is None else total + base
            if q < LAGMAX:
                heads.append(base[0:1])
            if q >= cols - LAGMAX:
                tails[cols - 1 - q] = base[7:8]
            for d in range(1, LAGMAX + 1):
                term = base * window[q + d]
                products[d - 1] = term if products[d - 1] is None else products[d - 1] + term
            if level + 1 < LEVELS:
                if q % 2 == 0:
                    previous = base
                else:
                    mean = (previous + base) * 0.5
                    level_ref[level, q // 2] = mean
                    if q // 2 < LAGMAX:
                        halo = jnp.where(sub < 7, pltpu.roll(mean, 7, 0), 0.0)
                        level_ref[level, cols // 2 + q // 2] = halo
        whole = jnp.sum(total, 0, keepdims=True)
        first, second = whole, whole
        for d in range(1, LAGMAX + 1):
            first = first - tails[d - 1]
            second = second - heads[d - 1]
            product = jnp.sum(products[d - 1], 0, keepdims=True)
            denom = first * second
            safe = jnp.where(denom > 0, denom, 1.0)
            value = jnp.where(denom > 0, product * float(length - d) / safe, 0.0)
            table_ref[level * LAGMAX + d - 1, pl.ds(b, 1), :] = value


def far_first(ny, nx):
    offsets = [(dy, dx, dc) for dy in range(ny) for dx in range(nx) for dc in range(2)][1:]
    order = []
    for dy, dx, dc in sorted(offsets, key=lambda o: -(min(o[0], ny - o[0]) + min(o[1], nx - o[1]))):
        for offset in ((dy, dx, dc), (-dy % ny, -dx % nx, dc)):
            if offset not in order:
                order.append(offset)
    return order


def core(
    ntm,
    nrows,
    lag_ref,
    owner_ref,
    slot_ref,
    frames_ref,
    g2_ref,
    two_ref,
    raw,
    flat,
    near_out,
    wide_out,
    wide_in,
    near_in,
    table_vec,
    table,
    pad_ref,
    level_ref,
    corr_ref,
    gram_ref,
    sums_ref,
    tall_ref,
    count_ref,
    own_buf,
    ratio_buf,
    out_buf,
    in_buf,
    local_sem,
    wide_send,
    wide_recv,
    near_send,
    near_recv,
    sum_send,
    sum_recv,
    ring_send,
    ring_recv,
):
    me = lax.axis_index("tm")
    row = lax.axis_index("rows")
    nx = 4
    ny = ntm // (2 * nx)
    barrier = pltpu.get_barrier_semaphore()
    load = pltpu.make_async_copy(frames_ref.at[:, 0], raw, local_sem.at[0])
    load.start()
    y, x, c = me // (2 * nx), (me // 2) % nx, me % 2

    def peer_at(offset):
        dy, dx, dc = offset
        return (lax.rem(y + dy, ny) * nx + lax.rem(x + dx, nx)) * 2 + lax.rem(c + dc, 2)

    def wrapped(value, size):
        return jnp.where(value >= size, value - size, value)

    for i in sorted(range(1, ntm), key=lambda i: -(min(i // 8, 4 - i // 8) + min(i // 2 % 4, 4 - i // 2 % 4))):
        peer = wrapped(me + i, ntm)
        pl.semaphore_signal(barrier, inc=1, device_id=(peer, row), device_id_type=MESH)
    for i in sorted(range(1, nrows), key=lambda i: -min(i, nrows - i)):
        peer = wrapped(row + i, nrows)
        pl.semaphore_signal(barrier, inc=1, device_id=(me, peer), device_id_type=MESH)

    span, nblocks, width = raw.shape
    halves, _, half = wide_in.shape[:3]
    slots = halves * half
    pitch = 16
    near = near_in.shape[1]
    square = (nblocks, nblocks)
    owners = owner_ref[pl.ds(row, 1), :].astype(jnp.float32)
    cycles = slot_ref[pl.ds(row, 1), :].astype(jnp.float32)
    down = lax.broadcasted_iota(jnp.int32, square, 0)
    along = lax.broadcasted_iota(jnp.int32, square, 1)
    alongf = along.astype(jnp.float32)
    across = jnp.broadcast_to(owners, square)
    same = (across == across.T) & (down < along)
    rank = jnp.sum(jnp.where(same, 1.0, 0.0), 0, keepdims=True)
    place = jnp.broadcast_to(owners * float(pitch) + rank, square).T
    entry = jnp.broadcast_to(alongf[0:1] + float(nblocks) * (1.0 + cycles), square).T
    parts = ntm * pitch // nblocks
    rows_of = [
        jnp.sum(jnp.where(place == alongf + float(j * nblocks), entry, 0.0), 0, keepdims=True)
        for j in range(parts)
    ]
    table_vec[...] = jnp.concatenate(
        rows_of + [jnp.zeros((8 - parts, nblocks), jnp.float32)], 0
    ).astype(jnp.int32)
    fetch = pltpu.make_async_copy(table_vec, table, local_sem.at[1])
    fetch.start()
    pad_ref[...] = jnp.zeros_like(pad_ref)
    load.wait()
    flat[...] = raw[...].astype(jnp.float32).reshape(span * nblocks, width)

    def turn(b, carry):
        near_out[b] = flat[pl.ds(b, span, stride=nblocks), :].astype(jnp.bfloat16)
        return carry

    lax.fori_loop(0, nblocks, turn, 0, unroll=8)
    fetch.wait()

    per = nblocks // pitch

    def entry_at(owner, k):
        return table[owner // per, (owner % per) * pitch + k]

    def fill(h):
        def place_owner(o, carry):
            tiles = [near_out[entry_at(o, h * half + k) & (nblocks - 1)] for k in range(half)]
            for k in range(half):
                wide_out[h, o, k] = tiles[k]
            return carry

        lax.fori_loop(0, ntm, place_owner, 0, unroll=2)
        wide_in[h, me] = wide_out[h, me]

    fill(0)
    near_in[me] = near_out[pl.ds(pl.multiple_of(me * near, near), near)]
    pl.semaphore_wait(barrier, ntm + nrows - 2)

    peers = [peer_at(offset) for offset in far_first(ny, nx)]

    def wide_copy(h, peer):
        return pltpu.make_async_remote_copy(
            src_ref=wide_out.at[h, peer],
            dst_ref=wide_in.at[h, me],
            send_sem=wide_send.at[h],
            recv_sem=wide_recv.at[h],
            device_id=(peer, row),
            device_id_type=MESH,
        )

    def near_copy(peer):
        return pltpu.make_async_remote_copy(
            src_ref=near_out.at[pl.ds(pl.multiple_of(peer * near, near), near)],
            dst_ref=near_in.at[me],
            send_sem=near_send.at[0],
            recv_sem=near_recv.at[0],
            device_id=(peer, row),
            device_id_type=MESH,
        )

    def batch(ref, send, recv):
        return pltpu.make_async_remote_copy(
            src_ref=ref.at[pl.ds(0, ntm - 1)],
            dst_ref=ref.at[pl.ds(0, ntm - 1)],
            send_sem=send,
            recv_sem=recv,
            device_id=(lax.rem(me + 1, ntm), row),
            device_id_type=MESH,
        )

    def wide_batch(h):
        return batch(wide_in.at[h], wide_send.at[h], wide_recv.at[h])

    near_batch = batch(near_in, near_send.at[0], near_recv.at[0])

    def sum_copy(i):
        peer = lax.rem(row + i, nrows)
        return pltpu.make_async_remote_copy(
            src_ref=sums_ref.at[row],
            dst_ref=sums_ref.at[row],
            send_sem=sum_send.at[0],
            recv_sem=sum_recv.at[row],
            device_id=(me, peer),
            device_id_type=MESH,
        )

    def sum_arrival(i):
        peer = lax.rem(row + i, nrows)
        return pltpu.make_async_remote_copy(
            src_ref=sums_ref.at[peer],
            dst_ref=sums_ref.at[peer],
            send_sem=sum_recv.at[peer],
            recv_sem=sum_recv.at[peer],
            device_id=(me, peer),
            device_id_type=MESH,
        )

    for h in range(halves):
        if h:
            fill(h)
        for peer in peers:
            wide_copy(h, peer).start()

    nf = ntm * span
    slab_len = nf // nrows
    contract = (((1,), (1,)), ((), ()))
    cycle_all = owner_ref[...] * 2 + slot_ref[...]
    group = lax.broadcasted_iota(jnp.int32, (nrows, nblocks), 0)
    distances = [lax.rem(row - group + nrows, nrows), lax.rem(group - row + nrows, nrows)]
    pixel_counts = [
        jnp.sum(jnp.where(cycle_all == me * 2 + a, float(width), 0.0), 1, keepdims=True) for a in range(2)
    ]

    def count_of(d, a, first, last):
        inside = (distances[d] >= first) & (distances[d] <= last)
        return jnp.sum(jnp.where(inside, pixel_counts[a], 0.0), 0, keepdims=True)

    def inverse(v):
        return jnp.where(v > 0, 1.0 / jnp.where(v > 0, v, 1.0), 0.0)

    for step in range(STEPS):
        before = [inverse(count_of(d, a, 1, step)) * (1.0 / CODE) for d in range(2) for a in range(2)]
        after = [count_of(d, a, 0, step) * CODE for d in range(2) for a in range(2)]
        count_ref[step] = jnp.concatenate(before + after, 0)
    before = [
        inverse(count_of(d, a, 1, STEPS - (d + a) % 2)) * (1.0 / CODE) for d in range(2) for a in range(2)
    ]
    whole = [count_of(0, a, 0, nrows) for a in range(2)]
    count_ref[STEPS] = jnp.concatenate(before + whole + whole, 0)

    own_entries = [entry_at(me, k) // nblocks for k in range(slots)]
    sums_own = None
    for h in range(halves):
        lines = [
            jnp.concatenate(
                [
                    jnp.full((1, width), jnp.where(e == a + 1, 1.0, 0.0), jnp.float32)
                    for e in own_entries[h * half : (h + 1) * half]
                ],
                1,
            )
            for a in range(2)
        ]
        masks = jnp.concatenate(lines + [jnp.zeros((14, half * width), jnp.float32)], 0)
        masks = masks.astype(jnp.bfloat16)
        wide_batch(h).wait_recv()
        pixels = jnp.concatenate([wide_in[h, :, k].reshape(nf, width) for k in range(half)], 1)
        left = jnp.concatenate([pixels * masks[0:1], pixels * masks[1:2], masks], 0)
        part = lax.dot_general(left, pixels, contract, preferred_element_type=jnp.float32)
        for a in range(2):
            term = part[a * nf : (a + 1) * nf]
            if h:
                gram_ref[a] += term
            else:
                gram_ref[a] = term
        term = part[2 * nf : 2 * nf + 2]
        sums_own = sums_own + term if h else term
    sums_ref[row] = sums_own
    for i in (1, nrows - 1):
        sum_copy(i).start()

    def sums_at(i):
        return sums_ref[lax.rem(row + i, nrows)]

    rows_len = slab_len // PIECES

    def rows_at(slab, piece):
        return pl.ds(pl.multiple_of(slab * slab_len + piece * rows_len, rows_len), rows_len)

    def tall_at(slab, piece, lane):
        return tall_ref[rows_at(slab, piece), lane : lane + 1]

    def own_part(a, slab, piece):
        return gram_ref[a, rows_at(slab, piece), :]

    def ring_copy(flow, step):
        _, way, _, _ = FLOWS[flow]
        return pltpu.make_async_remote_copy(
            src_ref=out_buf.at[FIRST[flow] + step],
            dst_ref=in_buf.at[FIRST[flow] + step],
            send_sem=ring_send.at[0],
            recv_sem=ring_recv.at[FIRST[flow] + step],
            device_id=(me, lax.rem(row + way + nrows, nrows)),
            device_id_type=MESH,
        )

    def tau(b, carry):
        multitau_block(b, near_in, pad_ref, level_ref, corr_ref)
        return carry

    up = jnp.zeros_like(sums_own)
    dn = jnp.zeros_like(sums_own)
    for step in range(STEPS):
        if step:
            sum_arrival(step).wait_recv()
            sum_arrival(nrows - step).wait_recv()
            up = up + sums_at(nrows - step)
            dn = dn + sums_at(step)
        lines = jnp.concatenate([up, dn, inverse(up + sums_own), inverse(dn + sums_own)], 0)
        tall_ref[...] = lines.T
        scaled = lines * count_ref[step][:, 0:1]

        live = [flow for flow in range(len(FLOWS)) if step < FLOWS[flow][2]]
        for flow in live:
            a, way, hops, piece = FLOWS[flow]
            slab = lax.rem(row + way * (hops - step) + nrows, nrows)
            lane = a if way > 0 else 2 + a
            tall = tall_at(slab, piece, lane + 4)
            line = scaled[lane + 4 : lane + 5]
            own = own_part(a, slab, piece) * tall * line + 0.5
            if step:
                ratio = (tall_at(slab, piece, lane) * tall) * (scaled[lane : lane + 1] * line)
                ratio_buf[flow] = ratio
                own_buf[flow] = own + ratio * float(BIAS)
            else:
                out_buf[FIRST[flow] + step] = (own.astype(jnp.int32) - BIAS).astype(jnp.int16)
                ring_copy(flow, step).start()
        if step:
            for flow in live:
                ring_copy(flow, step - 1).wait_recv()
                value = in_buf[FIRST[flow] + step - 1].astype(jnp.int32).astype(jnp.float32)
                code = (value * ratio_buf[flow] + own_buf[flow]).astype(jnp.int32) - BIAS
                out_buf[FIRST[flow] + step] = code.astype(jnp.int16)
                ring_copy(flow, step).start()

        if step == 0:
            for i in range(2, nrows - 1):
                sum_copy(i).start()
            for peer in peers:
                near_copy(peer).start()

    near_batch.wait_recv()
    lax.fori_loop(0, near, tau, 0)

    for l in range(LEVELS):
        for j in range(lag_ref.shape[1]):
            g2_ref[l * lag_ref.shape[1] + j] = corr_ref[
                l * LAGMAX + jnp.maximum(lag_ref[l, j] - 1, 0)
            ]
    sum_arrival(STEPS).wait_recv()
    last = sums_at(STEPS)
    sums = sums_own + up + dn + last
    ends = [up[0:1] + last[0:1], up[1:2], dn[0:1], dn[1:2] + last[1:2]]
    lines = jnp.concatenate(ends + [sums, sums], 0)
    tall_ref[...] = lines.T
    scaled = lines * count_ref[STEPS][:, 0:1]
    for piece in range(PIECES):
        for a in range(2):
            denom = jnp.maximum(tall_at(row, piece, 4 + a) * sums[a : a + 1], 1.0)
            weight = count_ref[STEPS, 4 + a : 5 + a, 0:1] / denom
            own = own_part(a, row, piece) * weight
            for d in range(2):
                flow = FLOWS.index((a, 1 - 2 * d, STEPS - (a + d) % 2, piece))
                lane = 2 * d + a
                ratio = tall_at(row, piece, lane) * scaled[lane : lane + 1] * weight
                ratio_buf[flow] = ratio
                own = own + ratio * float(BIAS)
            own_buf[FLOWS.index((a, 1, STEPS - a, piece))] = own
    for piece in range(PIECES):
        for a in range(2):
            value = own_buf[FLOWS.index((a, 1, STEPS - a, piece))]
            for hops in (STEPS - 1, STEPS):
                way = 1 if hops == STEPS - a else -1
                flow = FLOWS.index((a, way, hops, piece))
                ring_copy(flow, hops - 1).wait_recv()
                code = in_buf[FIRST[flow] + hops - 1].astype(jnp.int32).astype(jnp.float32)
                value = value + code * ratio_buf[flow]
            two_ref[pl.ds(piece * rows_len, rows_len), a, :] = value

    for h in range(halves):
        wide_batch(h).wait_send()
    near_batch.wait_send()
    for ref, sem, total in (
        (sums_ref, sum_send.at[0], nrows - 1),
        (out_buf, ring_send.at[0], MESSAGES),
    ):
        sent = ref.at[pl.ds(0, total)]
        pltpu.make_async_remote_copy(
            src_ref=sent,
            dst_ref=sent,
            send_sem=sem,
            recv_sem=sem,
            device_id=(me, lax.rem(row + 1, nrows)),
            device_id_type=MESH,
        ).wait_send()


def finish(g2_ref, two_ref, g2_out, two_out, sem):
    first = pltpu.make_async_copy(g2_ref, g2_out, sem.at[0])
    second = pltpu.make_async_copy(two_ref, two_out, sem.at[1])
    first.start()
    second.start()
    first.wait()
    second.wait()


def shards(frames, block_owner, cycle_slot, lag_table):
    span, _, nblocks, width = frames.shape
    ntm = lax.axis_size("tm")
    nrows = lax.axis_size("rows")
    cap = 3 * nblocks // ntm
    near = nblocks // ntm
    nf = span * ntm
    slab = nf // nrows
    nflow = len(FLOWS)
    vmem = pl.BlockSpec(memory_space=pltpu.VMEM)
    smem = pl.BlockSpec(memory_space=pltpu.SMEM)
    dma = pltpu.SemaphoreType.DMA
    bf16, f32, i32, i16 = jnp.bfloat16, jnp.float32, jnp.int32, jnp.int16
    g2, two = pl.pallas_call(
        functools.partial(core, ntm, nrows),
        out_shape=(
            pltpu.VMEM((LEVELS * lag_table.shape[1], near, width), f32),
            pltpu.VMEM((slab, 2, nf), f32),
        ),
        in_specs=[smem, vmem, vmem, pl.BlockSpec(memory_space=pl.ANY)],
        out_specs=(vmem, vmem),
        scratch_shapes=[
            pltpu.VMEM((span, nblocks, width), bf16),
            pltpu.VMEM((span * nblocks, width), f32),
            pltpu.VMEM((nblocks, span, width), bf16),
            pltpu.VMEM((2, ntm, cap // 2, span, width), bf16),
            pltpu.VMEM((2, ntm, cap // 2, span, width), bf16),
            pltpu.VMEM((ntm, near, span, width), bf16),
            pltpu.VMEM((8, nblocks), i32),
            pltpu.SMEM((8, nblocks), i32),
            pltpu.VMEM((nf + 64, width), f32),
            pltpu.VMEM((LEVELS - 1, nf // 16 + LAGMAX, 8, width), f32),
            pltpu.VMEM((LEVELS * LAGMAX, near, width), f32),
            pltpu.VMEM((2, nf, nf), f32),
            pltpu.VMEM((nrows, 2, nf), f32),
            pltpu.VMEM((nf, 8), f32),
            pltpu.VMEM((STEPS + 1, 8, nblocks), f32),
            pltpu.VMEM((nflow, slab // PIECES, nf), f32),
            pltpu.VMEM((nflow, slab // PIECES, nf), f32),
            pltpu.VMEM((MESSAGES, slab // PIECES, nf), i16),
            pltpu.VMEM((MESSAGES, slab // PIECES, nf), i16),
            dma((2,)),
            dma((2,)),
            dma((2,)),
            dma((1,)),
            dma((1,)),
            dma((1,)),
            dma((nrows,)),
            dma((1,)),
            dma((MESSAGES,)),
        ],
        compiler_params=pltpu.CompilerParams(collective_id=0, has_side_effects=True),
    )(lag_table, block_owner[:, :, 0], cycle_slot, frames)
    g2 = pltpu.with_memory_space_constraint(g2, pltpu.VMEM)
    two = pltpu.with_memory_space_constraint(two, pltpu.VMEM)
    hbm = pl.BlockSpec(memory_space=pl.ANY)
    g2, two = pl.pallas_call(
        finish,
        out_shape=(jax.ShapeDtypeStruct(g2.shape, f32), jax.ShapeDtypeStruct(two.shape, f32)),
        in_specs=[vmem, vmem],
        out_specs=(hbm, hbm),
        scratch_shapes=[dma((2,))],
    )(g2, two)
    return g2[None], two


def solution(mesh):
    in_specs = (P("tm", "rows", None, None), P(), P(), P())
    out_specs = (P("rows", None, "tm", None), P("rows", "tm", None))
    return jax.shard_map(shards, mesh=mesh, in_specs=in_specs, out_specs=out_specs, check_vma=False)
```

```python
import functools

import jax
import jax.numpy as jnp
from jax import lax
from jax.experimental import pallas as pl
from jax.experimental.pallas import tpu as pltpu
from jax.sharding import PartitionSpec as P

CYCLES = 64
LEVELS = 4
LAGMAX = 8
MESH = pl.DeviceIdType.MESH
PIECES = 2
CHAINS = ((0, 1, 4), (1, -1, 4), (0, -1, 3), (1, 1, 3))
FLOWS = tuple((a, way, hops, piece) for a, way, hops in CHAINS for piece in range(PIECES))
STEPS = 4
FIRST = tuple(sum(flow[2] for flow in FLOWS[:i]) for i in range(len(FLOWS) + 1))
MESSAGES = FIRST[-1]
CODE = 14500.0
BIAS = 32767


def multitau_block(b, recv_ref, pad_ref, level_ref, table_ref):
    nf = recv_ref.shape[0] * recv_ref.shape[2]
    width = recv_ref.shape[3]
    pad_ref[pl.ds(0, nf), :] = recv_ref[:, b].astype(jnp.float32).reshape(nf, width)
    sub = lax.broadcasted_iota(jnp.int32, (8, width), 0)
    for level in range(LEVELS):
        length = nf >> level
        cols = length // 8

        def get(q, level=level, cols=cols):
            if level == 0:
                return pad_ref[pl.ds(q, 8, stride=cols), :]
            return level_ref[level - 1, q]

        window = [get(q) for q in range(LAGMAX)]
        products = [None] * LAGMAX
        total = None
        heads = []
        tails = [None] * LAGMAX
        previous = None
        for q in range(cols):
            window.append(get(q + LAGMAX))
            base = window[q]
            total = base if total is None else total + base
            if q < LAGMAX:
                heads.append(base[0:1])
            if q >= cols - LAGMAX:
                tails[cols - 1 - q] = base[7:8]
            for d in range(1, LAGMAX + 1):
                term = base * window[q + d]
                products[d - 1] = term if products[d - 1] is None else products[d - 1] + term
            if level + 1 < LEVELS:
                if q % 2 == 0:
                    previous = base
                else:
                    mean = (previous + base) * 0.5
                    level_ref[level, q // 2] = mean
                    if q // 2 < LAGMAX:
                        halo = jnp.where(sub < 7, pltpu.roll(mean, 7, 0), 0.0)
                        level_ref[level, cols // 2 + q // 2] = halo
        whole = jnp.sum(total, 0, keepdims=True)
        first, second = whole, whole
        for d in range(1, LAGMAX + 1):
            first = first - tails[d - 1]
            second = second - heads[d - 1]
            product = jnp.sum(products[d - 1], 0, keepdims=True)
            denom = first * second
            safe = jnp.where(denom > 0, denom, 1.0)
            value = jnp.where(denom > 0, product * float(length - d) / safe, 0.0)
            table_ref[level * LAGMAX + d - 1, pl.ds(b, 1), :] = value


def far_first(ny, nx):
    offsets = [(dy, dx, dc) for dy in range(ny) for dx in range(nx) for dc in range(2)][1:]
    order = []
    for dy, dx, dc in sorted(offsets, key=lambda o: -(min(o[0], ny - o[0]) + min(o[1], nx - o[1]))):
        for offset in ((dy, dx, dc), (-dy % ny, -dx % nx, dc)):
            if offset not in order:
                order.append(offset)
    return order


def core(
    ntm,
    nrows,
    lag_ref,
    owner_ref,
    slot_ref,
    frames_ref,
    g2_ref,
    two_ref,
    raw,
    flat,
    near_out,
    wide_out,
    wide_in,
    near_in,
    table_vec,
    table,
    pad_ref,
    level_ref,
    corr_ref,
    gram_ref,
    sums_ref,
    tall_ref,
    count_ref,
    own_buf,
    ratio_buf,
    out_buf,
    in_buf,
    local_sem,
    wide_send,
    wide_recv,
    near_send,
    near_recv,
    sum_send,
    sum_recv,
    ring_send,
    ring_recv,
):
    me = lax.axis_index("tm")
    row = lax.axis_index("rows")
    nx = 4
    ny = ntm // (2 * nx)
    barrier = pltpu.get_barrier_semaphore()
    load = pltpu.make_async_copy(frames_ref.at[:, 0], raw, local_sem.at[0])
    load.start()
    y, x, c = me // (2 * nx), (me // 2) % nx, me % 2

    def peer_at(offset):
        dy, dx, dc = offset
        return (lax.rem(y + dy, ny) * nx + lax.rem(x + dx, nx)) * 2 + lax.rem(c + dc, 2)

    def wrapped(value, size):
        return jnp.where(value >= size, value - size, value)

    for i in sorted(range(1, ntm), key=lambda i: -(min(i // 8, 4 - i // 8) + min(i // 2 % 4, 4 - i // 2 % 4))):
        peer = wrapped(me + i, ntm)
        pl.semaphore_signal(barrier, inc=1, device_id=(peer, row), device_id_type=MESH)
    for i in sorted(range(1, nrows), key=lambda i: -min(i, nrows - i)):
        peer = wrapped(row + i, nrows)
        pl.semaphore_signal(barrier, inc=1, device_id=(me, peer), device_id_type=MESH)

    span, nblocks, width = raw.shape
    halves, _, half = wide_in.shape[:3]
    slots = halves * half
    pitch = 16
    near = near_in.shape[1]
    square = (nblocks, nblocks)
    owners = owner_ref[pl.ds(row, 1), :].astype(jnp.float32)
    cycles = slot_ref[pl.ds(row, 1), :].astype(jnp.float32)
    down = lax.broadcasted_iota(jnp.int32, square, 0)
    along = lax.broadcasted_iota(jnp.int32, square, 1)
    alongf = along.astype(jnp.float32)
    across = jnp.broadcast_to(owners, square)
    same = (across == across.T) & (down < along)
    rank = jnp.sum(jnp.where(same, 1.0, 0.0), 0, keepdims=True)
    place = jnp.broadcast_to(owners * float(pitch) + rank, square).T
    entry = jnp.broadcast_to(alongf[0:1] + float(nblocks) * (1.0 + cycles), square).T
    parts = ntm * pitch // nblocks
    rows_of = [
        jnp.sum(jnp.where(place == alongf + float(j * nblocks), entry, 0.0), 0, keepdims=True)
        for j in range(parts)
    ]
    table_vec[...] = jnp.concatenate(
        rows_of + [jnp.zeros((8 - parts, nblocks), jnp.float32)], 0
    ).astype(jnp.int32)
    fetch = pltpu.make_async_copy(table_vec, table, local_sem.at[1])
    fetch.start()
    pad_ref[...] = jnp.zeros_like(pad_ref)
    load.wait()
    flat[...] = raw[...].astype(jnp.float32).reshape(span * nblocks, width)

    def turn(b, carry):
        near_out[b] = flat[pl.ds(b, span, stride=nblocks), :].astype(jnp.bfloat16)
        return carry

    lax.fori_loop(0, nblocks, turn, 0, unroll=8)
    fetch.wait()

    per = nblocks // pitch

    def entry_at(owner, k):
        return table[owner // per, (owner % per) * pitch + k]

    def fill(h):
        def place_owner(o, carry):
            tiles = [near_out[entry_at(o, h * half + k) & (nblocks - 1)] for k in range(half)]
            for k in range(half):
                wide_out[h, o, k] = tiles[k]
            return carry

        lax.fori_loop(0, ntm, place_owner, 0, unroll=2)
        wide_in[h, me] = wide_out[h, me]

    fill(0)
    near_in[me] = near_out[pl.ds(pl.multiple_of(me * near, near), near)]
    pl.semaphore_wait(barrier, ntm + nrows - 2)

    peers = [peer_at(offset) for offset in far_first(ny, nx)]

    def wide_copy(h, peer):
        return pltpu.make_async_remote_copy(
            src_ref=wide_out.at[h, peer],
            dst_ref=wide_in.at[h, me],
            send_sem=wide_send.at[h],
            recv_sem=wide_recv.at[h],
            device_id=(peer, row),
            device_id_type=MESH,
        )

    def near_copy(peer):
        return pltpu.make_async_remote_copy(
            src_ref=near_out.at[pl.ds(pl.multiple_of(peer * near, near), near)],
            dst_ref=near_in.at[me],
            send_sem=near_send.at[0],
            recv_sem=near_recv.at[0],
            device_id=(peer, row),
            device_id_type=MESH,
        )

    def batch(ref, send, recv):
        return pltpu.make_async_remote_copy(
            src_ref=ref.at[pl.ds(0, ntm - 1)],
            dst_ref=ref.at[pl.ds(0, ntm - 1)],
            send_sem=send,
            recv_sem=recv,
            device_id=(lax.rem(me + 1, ntm), row),
            device_id_type=MESH,
        )

    def wide_batch(h):
        return batch(wide_in.at[h], wide_send.at[h], wide_recv.at[h])

    near_batch = batch(near_in, near_send.at[0], near_recv.at[0])

    def sum_copy(i):
        peer = lax.rem(row + i, nrows)
        return pltpu.make_async_remote_copy(
            src_ref=sums_ref.at[row],
            dst_ref=sums_ref.at[row],
            send_sem=sum_send.at[0],
            recv_sem=sum_recv.at[row],
            device_id=(me, peer),
            device_id_type=MESH,
        )

    def sum_arrival(i):
        peer = lax.rem(row + i, nrows)
        return pltpu.make_async_remote_copy(
            src_ref=sums_ref.at[peer],
            dst_ref=sums_ref.at[peer],
            send_sem=sum_recv.at[peer],
            recv_sem=sum_recv.at[peer],
            device_id=(me, peer),
            device_id_type=MESH,
        )

    for h in range(halves):
        if h:
            fill(h)
        for peer in peers:
            wide_copy(h, peer).start()

    nf = ntm * span
    slab_len = nf // nrows
    contract = (((1,), (1,)), ((), ()))
    cycle_all = owner_ref[...] * 2 + slot_ref[...]
    group = lax.broadcasted_iota(jnp.int32, (nrows, nblocks), 0)
    distances = [lax.rem(row - group + nrows, nrows), lax.rem(group - row + nrows, nrows)]
    pixel_counts = [
        jnp.sum(jnp.where(cycle_all == me * 2 + a, float(width), 0.0), 1, keepdims=True) for a in range(2)
    ]

    def count_of(d, a, first, last):
        inside = (distances[d] >= first) & (distances[d] <= last)
        return jnp.sum(jnp.where(inside, pixel_counts[a], 0.0), 0, keepdims=True)

    def inverse(v):
        return jnp.where(v > 0, 1.0 / jnp.where(v > 0, v, 1.0), 0.0)

    for step in range(STEPS):
        before = [inverse(count_of(d, a, 1, step)) * (1.0 / CODE) for d in range(2) for a in range(2)]
        after = [count_of(d, a, 0, step) * CODE for d in range(2) for a in range(2)]
        count_ref[step] = jnp.concatenate(before + after, 0)
    before = [
        inverse(count_of(d, a, 1, STEPS - (d + a) % 2)) * (1.0 / CODE) for d in range(2) for a in range(2)
    ]
    whole = [count_of(0, a, 0, nrows) for a in range(2)]
    count_ref[STEPS] = jnp.concatenate(before + whole + whole, 0)

    own_entries = [entry_at(me, k) // nblocks for k in range(slots)]
    sums_own = None
    for h in range(halves):
        lines = [
            jnp.concatenate(
                [
                    jnp.full((1, width), jnp.where(e == a + 1, 1.0, 0.0), jnp.float32)
                    for e in own_entries[h * half : (h + 1) * half]
                ],
                1,
            )
            for a in range(2)
        ]
        masks = jnp.concatenate(lines + [jnp.zeros((14, half * width), jnp.float32)], 0)
        masks = masks.astype(jnp.bfloat16)
        wide_batch(h).wait_recv()
        pixels = jnp.concatenate([wide_in[h, :, k].reshape(nf, width) for k in range(half)], 1)
        left = jnp.concatenate([pixels * masks[0:1], pixels * masks[1:2], masks], 0)
        part = lax.dot_general(left, pixels, contract, preferred_element_type=jnp.float32)
        for a in range(2):
            term = part[a * nf : (a + 1) * nf]
            if h:
                gram_ref[a] += term
            else:
                gram_ref[a] = term
        term = part[2 * nf : 2 * nf + 2]
        sums_own = sums_own + term if h else term
    sums_ref[row] = sums_own
    for i in (1, nrows - 1):
        sum_copy(i).start()

    def sums_at(i):
        return sums_ref[lax.rem(row + i, nrows)]

    rows_len = slab_len // PIECES

    def rows_at(slab, piece):
        return pl.ds(pl.multiple_of(slab * slab_len + piece * rows_len, rows_len), rows_len)

    def tall_at(slab, piece, lane):
        return tall_ref[rows_at(slab, piece), lane : lane + 1]

    def own_part(a, slab, piece):
        return gram_ref[a, rows_at(slab, piece), :]

    def ring_copy(flow, step):
        _, way, _, _ = FLOWS[flow]
        return pltpu.make_async_remote_copy(
            src_ref=out_buf.at[FIRST[flow] + step],
            dst_ref=in_buf.at[FIRST[flow] + step],
            send_sem=ring_send.at[0],
            recv_sem=ring_recv.at[FIRST[flow] + step],
            device_id=(me, lax.rem(row + way + nrows, nrows)),
            device_id_type=MESH,
        )

    def tau(b, carry):
        multitau_block(b, near_in, pad_ref, level_ref, corr_ref)
        return carry

    up = jnp.zeros_like(sums_own)
    dn = jnp.zeros_like(sums_own)
    for step in range(STEPS):
        if step:
            sum_arrival(step).wait_recv()
            sum_arrival(nrows - step).wait_recv()
            up = up + sums_at(nrows - step)
            dn = dn + sums_at(step)
        lines = jnp.concatenate([up, dn, inverse(up + sums_own), inverse(dn + sums_own)], 0)
        tall_ref[...] = lines.T
        scaled = lines * count_ref[step][:, 0:1]

        live = [flow for flow in range(len(FLOWS)) if step < FLOWS[flow][2]]
        for flow in live:
            a, way, hops, piece = FLOWS[flow]
            slab = lax.rem(row + way * (hops - step) + nrows, nrows)
            lane = a if way > 0 else 2 + a
            tall = tall_at(slab, piece, lane + 4)
            line = scaled[lane + 4 : lane + 5]
            own = own_part(a, slab, piece) * tall * line + 0.5
            if step:
                ratio = (tall_at(slab, piece, lane) * tall) * (scaled[lane : lane + 1] * line)
                ratio_buf[flow] = ratio
                own_buf[flow] = own + ratio * float(BIAS)
            else:
                out_buf[FIRST[flow] + step] = (own.astype(jnp.int32) - BIAS).astype(jnp.int16)
                ring_copy(flow, step).start()
        def serve(first, step=step, live=live):
            for flow in sorted(live, key=lambda f: (-FLOWS[f][2], FLOWS[f][1] != first, f)):
                ring_copy(flow, step - 1).wait_recv()
                value = in_buf[FIRST[flow] + step - 1].astype(jnp.int32).astype(jnp.float32)
                code = (value * ratio_buf[flow] + own_buf[flow]).astype(jnp.int32) - BIAS
                out_buf[FIRST[flow] + step] = code.astype(jnp.int16)
                ring_copy(flow, step).start()

        if step:
            rising = lax.rem(row, STEPS) >= STEPS // 2
            pl.when(rising)(functools.partial(serve, 1))
            pl.when(jnp.logical_not(rising))(functools.partial(serve, -1))
        if step == 0:
            for i in range(2, nrows - 1):
                sum_copy(i).start()
            for peer in peers:
                near_copy(peer).start()

    near_batch.wait_recv()
    lax.fori_loop(0, near, tau, 0)

    for l in range(LEVELS):
        for j in range(lag_ref.shape[1]):
            g2_ref[l * lag_ref.shape[1] + j] = corr_ref[
                l * LAGMAX + jnp.maximum(lag_ref[l, j] - 1, 0)
            ]
    sum_arrival(STEPS).wait_recv()
    last = sums_at(STEPS)
    sums = sums_own + up + dn + last
    ends = [up[0:1] + last[0:1], up[1:2], dn[0:1], dn[1:2] + last[1:2]]
    lines = jnp.concatenate(ends + [sums, sums], 0)
    tall_ref[...] = lines.T
    scaled = lines * count_ref[STEPS][:, 0:1]
    for piece in range(PIECES):
        for a in range(2):
            denom = jnp.maximum(tall_at(row, piece, 4 + a) * sums[a : a + 1], 1.0)
            weight = count_ref[STEPS, 4 + a : 5 + a, 0:1] / denom
            own = own_part(a, row, piece) * weight
            for d in range(2):
                flow = FLOWS.index((a, 1 - 2 * d, STEPS - (a + d) % 2, piece))
                lane = 2 * d + a
                ratio = tall_at(row, piece, lane) * scaled[lane : lane + 1] * weight
                ratio_buf[flow] = ratio
                own = own + ratio * float(BIAS)
            own_buf[FLOWS.index((a, 1, STEPS - a, piece))] = own
    for piece in range(PIECES):
        for a in range(2):
            value = own_buf[FLOWS.index((a, 1, STEPS - a, piece))]
            for hops in (STEPS - 1, STEPS):
                way = 1 if hops == STEPS - a else -1
                flow = FLOWS.index((a, way, hops, piece))
                ring_copy(flow, hops - 1).wait_recv()
                code = in_buf[FIRST[flow] + hops - 1].astype(jnp.int32).astype(jnp.float32)
                value = value + code * ratio_buf[flow]
            two_ref[pl.ds(piece * rows_len, rows_len), a, :] = value

    for h in range(halves):
        wide_batch(h).wait_send()
    near_batch.wait_send()
    for ref, sem, total in (
        (sums_ref, sum_send.at[0], nrows - 1),
        (out_buf, ring_send.at[0], MESSAGES),
    ):
        sent = ref.at[pl.ds(0, total)]
        pltpu.make_async_remote_copy(
            src_ref=sent,
            dst_ref=sent,
            send_sem=sem,
            recv_sem=sem,
            device_id=(me, lax.rem(row + 1, nrows)),
            device_id_type=MESH,
        ).wait_send()


def finish(g2_ref, two_ref, g2_out, two_out, sem):
    first = pltpu.make_async_copy(g2_ref, g2_out, sem.at[0])
    second = pltpu.make_async_copy(two_ref, two_out, sem.at[1])
    first.start()
    second.start()
    first.wait()
    second.wait()


def shards(frames, block_owner, cycle_slot, lag_table):
    span, _, nblocks, width = frames.shape
    ntm = lax.axis_size("tm")
    nrows = lax.axis_size("rows")
    cap = 3 * nblocks // ntm
    near = nblocks // ntm
    nf = span * ntm
    slab = nf // nrows
    nflow = len(FLOWS)
    vmem = pl.BlockSpec(memory_space=pltpu.VMEM)
    smem = pl.BlockSpec(memory_space=pltpu.SMEM)
    dma = pltpu.SemaphoreType.DMA
    bf16, f32, i32, i16 = jnp.bfloat16, jnp.float32, jnp.int32, jnp.int16
    g2, two = pl.pallas_call(
        functools.partial(core, ntm, nrows),
        out_shape=(
            pltpu.VMEM((LEVELS * lag_table.shape[1], near, width), f32),
            pltpu.VMEM((slab, 2, nf), f32),
        ),
        in_specs=[smem, vmem, vmem, pl.BlockSpec(memory_space=pl.ANY)],
        out_specs=(vmem, vmem),
        scratch_shapes=[
            pltpu.VMEM((span, nblocks, width), bf16),
            pltpu.VMEM((span * nblocks, width), f32),
            pltpu.VMEM((nblocks, span, width), bf16),
            pltpu.VMEM((2, ntm, cap // 2, span, width), bf16),
            pltpu.VMEM((2, ntm, cap // 2, span, width), bf16),
            pltpu.VMEM((ntm, near, span, width), bf16),
            pltpu.VMEM((8, nblocks), i32),
            pltpu.SMEM((8, nblocks), i32),
            pltpu.VMEM((nf + 64, width), f32),
            pltpu.VMEM((LEVELS - 1, nf // 16 + LAGMAX, 8, width), f32),
            pltpu.VMEM((LEVELS * LAGMAX, near, width), f32),
            pltpu.VMEM((2, nf, nf), f32),
            pltpu.VMEM((nrows, 2, nf), f32),
            pltpu.VMEM((nf, 8), f32),
            pltpu.VMEM((STEPS + 1, 8, nblocks), f32),
            pltpu.VMEM((nflow, slab // PIECES, nf), f32),
            pltpu.VMEM((nflow, slab // PIECES, nf), f32),
            pltpu.VMEM((MESSAGES, slab // PIECES, nf), i16),
            pltpu.VMEM((MESSAGES, slab // PIECES, nf), i16),
            dma((2,)),
            dma((2,)),
            dma((2,)),
            dma((1,)),
            dma((1,)),
            dma((1,)),
            dma((nrows,)),
            dma((1,)),
            dma((MESSAGES,)),
        ],
        compiler_params=pltpu.CompilerParams(collective_id=0, has_side_effects=True),
    )(lag_table, block_owner[:, :, 0], cycle_slot, frames)
    g2 = pltpu.with_memory_space_constraint(g2, pltpu.VMEM)
    two = pltpu.with_memory_space_constraint(two, pltpu.VMEM)
    hbm = pl.BlockSpec(memory_space=pl.ANY)
    g2, two = pl.pallas_call(
        finish,
        out_shape=(jax.ShapeDtypeStruct(g2.shape, f32), jax.ShapeDtypeStruct(two.shape, f32)),
        in_specs=[vmem, vmem],
        out_specs=(hbm, hbm),
        scratch_shapes=[dma((2,))],
    )(g2, two)
    return g2[None], two


def solution(mesh):
    in_specs = (P("tm", "rows", None, None), P(), P(), P())
    out_specs = (P("rows", None, "tm", None), P("rows", "tm", None))
    return jax.shard_map(shards, mesh=mesh, in_specs=in_specs, out_specs=out_specs, check_vma=False)
```
